32 devices in a mesh: row: 8 (over y, x, core), col: 4 (over z).
Axes of the slice: x: 2, y: 2, z: 4, core: 2. Of those that a mesh axis runs over, the one named last changes fastest.
Arguments:
- images: bfloat16 [16384, 768], P(('row', 'col')), may hold values from -2 to 2
- weight_in: bfloat16 [768, 2048], replicated, may hold values from -0.21875 to 0.21875
- bias_in: float32 [2048], replicated, may hold values from -3 to 3
- weight_out: bfloat16 [2048, 256], replicated, may hold values from -0.125 to 0.125
- feature_scale: float32 [256], replicated, may hold values from 0.05 to 0.25
- position: int32 [16384], P(('row', 'col')), may hold values from 0 to 16383, as said below
Outputs:
- panel_tiles: float32 [16, 1024, 2, 512], P(None, 'row', None, 'col')
- next_tiles: float32 [16, 1024, 2, 512], P(None, 'row', None, 'col')
The draws below stay inside these ranges and needn't reach their ends.
Inputs may be any that keep to these rules, and one draw needn't show every extreme that they name: position is a permutation of the kernel rows. Among the images of one device (each aligned block of 512 images) exactly 64 have a position whose tile index, position // 128, leaves a given remainder modulo the number of devices along row, for every remainder.
All inputs are finite; a program needn't handle non-finite values.
Results may differ from the reference program's by a relative error of at most 0.0057.
Values may be sent and summed in bfloat16 or wider, within the bound.
No kernel may reach another device: no remote copies, remote signals or barrier semaphores. Data moves between devices by JAX's collectives and lax.ppermute only.
A program may use at most 128 MiB of HBM per device.

```python
import math
import jax
import jax.numpy as jnp
from jax import lax

DIN = 768
HID = 2048
FEAT = 256
TILE = 128
PANEL = 1024
IMG_DEV = 512
IMAGES = 16384
SHARE = 64
LOCAL_TILES = 16
COL_TILES = 2
N_ROW = 8
N_COL = 4
DEVICES = 32


def draw_position(key, part):
    per_group = IMAGES // N_ROW

    def group_places(group_id):
        shuffled = jax.random.permutation(jax.random.fold_in(key, group_id), per_group)
        return (shuffled // TILE * N_ROW + group_id) * TILE + shuffled % TILE
    table = jax.vmap(group_places)(jnp.arange(N_ROW))
    table = table.reshape(N_ROW, DEVICES, SHARE).transpose(1, 0, 2).reshape(DEVICES, IMG_DEV)

    def shuffle_block(block_row, block_id):
        return jax.random.permutation(jax.random.fold_in(key, 7919 + block_id), block_row)
    mixed = jax.vmap(shuffle_block)(table, jnp.arange(DEVICES))
    return mixed.reshape(IMAGES).astype(jnp.int32)


def draw_images(key, part):
    latent_key = jax.random.fold_in(key, 101)
    freq_key = jax.random.fold_in(key, 202)
    phase_key = jax.random.fold_in(key, 303)
    jitter_key = jax.random.fold_in(key, 404)
    latent = jax.random.normal(latent_key, (IMAGES, 8), jnp.float32)
    jitter = jnp.clip(0.1 * jax.random.normal(jitter_key, (IMAGES, DIN), jnp.float32), -0.5, 0.5)
    amplitude = 1.4
    log_freq = jax.random.uniform(freq_key, (DIN,), jnp.float32, jnp.log(0.6), jnp.log(2.5))
    freqs = jnp.exp(log_freq)
    phases = jax.random.uniform(phase_key, (DIN,), jnp.float32, -jnp.pi, jnp.pi)
    spread = jnp.broadcast_to(latent[:, None, :], (IMAGES, DIN // 8, 8)).reshape(IMAGES, DIN)
    values = amplitude * jnp.cos(freqs[None, :] * spread + phases[None, :]) + jitter
    return jnp.clip(values, -2.0, 2.0).astype(jnp.bfloat16)


def centred(own_key, shape, deviation, most, kind=jnp.bfloat16):
    drawn = deviation * jax.random.normal(own_key, shape, jnp.float32)
    return jnp.clip(drawn, min=-most, max=most).astype(kind)


def setup_inputs(seed: int = 0) -> dict:
    key_list = jax.random.split(jax.random.key(seed), 7)
    images = draw_images(jax.random.fold_in(key_list[6], 71), 0)
    weight_in = centred(key_list[1], (DIN, HID), DIN ** -0.5, 0.21875)
    bias_in = centred(key_list[2], (HID,), 0.5, 3.0, jnp.float32)
    weight_out = centred(key_list[3], (HID, FEAT), HID ** -0.5, 0.125)
    feature_scale = jnp.clip(jnp.exp(jax.random.uniform(key_list[4], (FEAT,), jnp.float32, math.log(0.05), math.log(0.25))), 0.05, 0.25)
    position = draw_position(jax.random.fold_in(key_list[6], 71), 0)
    return {"images": images, "weight_in": weight_in, "bias_in": bias_in, "weight_out": weight_out, "feature_scale": feature_scale, "position": position}


noise_var = 0.5

def kernel_block(left_feats, right_feats):
    left_norm = jnp.sum(jnp.square(left_feats.astype(jnp.float32)), axis=1)
    right_norm = jnp.sum(jnp.square(right_feats.astype(jnp.float32)), axis=1)
    cross_block = jnp.dot(left_feats.astype(jnp.float32), right_feats.T.astype(jnp.float32), preferred_element_type=jnp.float32)
    distance = left_norm[:, None] + right_norm[None, :] - 2.0 * cross_block
    return jnp.exp(-0.5 * jnp.maximum(distance, 0.0))

def reference(images, weight_in, bias_in, weight_out, feature_scale, position):
    preact = jnp.dot(images.astype(jnp.float32), weight_in.astype(jnp.float32), preferred_element_type=jnp.float32) + bias_in.astype(jnp.float32)
    hidden = jax.nn.gelu(preact, approximate=True).astype(jnp.bfloat16)
    features = (jnp.dot(hidden.astype(jnp.float32), weight_out.astype(jnp.float32), preferred_element_type=jnp.float32) * feature_scale).astype(jnp.bfloat16)
    ordered = jnp.zeros_like(features).at[position].set(features)
    columns = ordered[:2 * PANEL]
    kernel = kernel_block(ordered, columns)
    row_place = jnp.arange(IMAGES)[:, None]
    col_place = jnp.arange(2 * PANEL)[None, :]
    kernel = kernel + jnp.where(row_place == col_place, noise_var, 0.0).astype(kernel.dtype)
    factor = jnp.linalg.cholesky(kernel[:PANEL, :PANEL])
    identity = jnp.eye(PANEL, dtype=jnp.float32).astype(kernel.dtype)
    inverse_t = jax.scipy.linalg.solve_triangular(factor, identity, lower=True, trans=1)
    panel_full = jnp.dot(kernel[:, :PANEL], inverse_t, precision=lax.Precision.HIGHEST)
    update = kernel[:, PANEL:] - jnp.dot(panel_full, panel_full[PANEL:2 * PANEL].T, precision=lax.Precision.HIGHEST)
    shape_out = (LOCAL_TILES, N_ROW * TILE, COL_TILES, N_COL * TILE)
    return (panel_full.reshape(shape_out), update.reshape(shape_out))
```

```python
import functools

import jax
import jax.numpy as jnp
from jax import lax
from jax.experimental import pallas as pl
from jax.experimental.pallas import tpu as pltpu
from jax.sharding import PartitionSpec as P

TILE = 128
PANEL = 1024
META = 16
F32 = jnp.float32
BF16 = jnp.bfloat16
NN = (((1,), (0,)), ((), ()))
NT = (((1,), (1,)), ((), ()))
TN = (((0,), (0,)), ((), ()))

noise_var = 0.5


def iota(shape, dim):
    return lax.broadcasted_iota(jnp.int32, shape, dim)


def one_hot(cond):
    return jnp.where(cond, 1.0, 0.0).astype(BF16)


def dot(left, right, dims=NN):
    return lax.dot_general(left, right, dims, preferred_element_type=F32)


def split(value):
    high = value.astype(BF16)
    return high, (value - high.astype(F32)).astype(BF16)


def dot_split(left, right, dims=NN):
    return dot(left[0], right[0], dims) + (
        dot(left[0], right[1], dims) + dot(left[1], right[0], dims)
    )


def half_norms(feats):
    wide = feats.astype(F32)
    return 0.5 * jnp.sum(wide * wide, axis=1, keepdims=True)


def as_row(column):
    rows = column.shape[0]
    return jnp.broadcast_to(column, (rows, TILE)).T[:1, :]


def rbf(left, left_half, right, right_half_row):
    cross = dot(left, right, NT)
    return jnp.exp(jnp.minimum(cross - left_half - right_half_row, 0.0))


def feature_kernel(
    share, row_count, pos_ref, img_ref, win_ref, bias_ref, wout_ref, scale_ref, out_ref, acc_ref
):
    step = pl.program_id(0)
    preact = dot(img_ref[...], win_ref[...]) + bias_ref[...]
    hidden = 0.5 * preact * (1.0 + jnp.tanh(0.7978845608 * (preact + 0.044715 * preact * preact * preact)))
    part = dot(hidden.astype(BF16), wout_ref[...])

    @pl.when(step == 0)
    def _():
        acc_ref[...] = part

    @pl.when(step > 0)
    def _():
        acc_ref[...] += part

    @pl.when(step == pl.num_programs(0) - 1)
    def _():
        images = row_count * share
        feats = (acc_ref[...] * scale_ref[...]).astype(BF16)
        place = pos_ref[...]
        tile = place // TILE
        group = tile % row_count
        member = iota((row_count, images), 0) == group
        before = one_hot(iota((images, images), 0) < iota((images, images), 1))
        rank = dot(one_hot(member), before)
        target = jnp.where(member, rank + (share * iota((row_count, images), 0)).astype(F32), 0.0)
        target = jnp.sum(target, axis=0, keepdims=True).astype(jnp.int32)
        order = one_hot(iota((images, images), 0) == target)
        sorted_feats = dot(order, feats).astype(BF16)
        meta_row = iota((META, images), 0)
        meta = jnp.where(meta_row == 0, tile // row_count, jnp.where(meta_row == 1, place % TILE, 0))
        meta = meta.astype(F32).astype(BF16)
        lane = iota((TILE, images), 0) % share
        for r in range(row_count):
            out_ref[r, :share, :] = sorted_feats[r * share : (r + 1) * share, :]
            sel = one_hot(lane + r * share == target)
            spread = dot(meta, sel, NT).astype(BF16)
            out_ref[r, share:, :TILE] = spread
            out_ref[r, share:, TILE:] = jnp.zeros((META, out_ref.shape[2] - TILE), BF16)


def make_features(images, weight_in, bias_in, weight_out, feature_scale, position, row_count):
    rows, din = images.shape
    hid, feat = weight_out.shape
    share = rows // row_count
    block = 512
    return pl.pallas_call(
        functools.partial(feature_kernel, share, row_count),
        out_shape=jax.ShapeDtypeStruct((row_count, share + META, feat), BF16),
        grid=(hid // block,),
        in_specs=[
            pl.BlockSpec((1, rows), lambda i: (0, 0)),
            pl.BlockSpec((rows, din), lambda i: (0, 0)),
            pl.BlockSpec((din, block), lambda i: (0, i)),
            pl.BlockSpec((1, block), lambda i: (0, i)),
            pl.BlockSpec((block, feat), lambda i: (i, 0)),
            pl.BlockSpec((1, feat), lambda i: (0, 0)),
        ],
        out_specs=pl.BlockSpec((row_count, share + META, feat), lambda i: (0, 0, 0)),
        scratch_shapes=[pltpu.VMEM((rows, feat), F32)],
        compiler_params=pltpu.CompilerParams(vmem_limit_bytes=32 << 20),
        name="features",
    )(
        position.reshape(1, rows),
        images,
        weight_in,
        bias_in.reshape(1, hid),
        weight_out,
        feature_scale.reshape(1, feat),
    )


def read_slots(block_ref, lead, share, group):
    per = TILE // share
    lane = iota((META, TILE), 1) // share
    meta = None
    for j in range(per):
        piece = block_ref[lead + (group * per + j, slice(share, share + META), slice(0, TILE))].astype(F32)
        meta = piece if meta is None else jnp.where(lane == j, piece, meta)
    return (meta[0:1, :] * TILE + meta[1:2, :]).astype(jnp.int32)


def gather_rows(block_ref, lead, share, group):
    per = TILE // share
    return jnp.concatenate(
        [block_ref[lead + (group * per + j, slice(0, share), slice(None))] for j in range(per)], axis=0
    )


def lead_kernel(share, recv_ref, *out_refs):
    groups = recv_ref.shape[0] * share // TILE
    slots = [read_slots(recv_ref, (), share, g) for g in range(groups)]
    rows = jnp.concatenate([gather_rows(recv_ref, (), share, g) for g in range(groups)], axis=0)
    for t, out_ref in enumerate(out_refs):
        pick = jnp.concatenate(
            [one_hot(iota((TILE, TILE), 0) + t * TILE == s) for s in slots], axis=1
        )
        out_ref[...] = dot(pick, rows).astype(BF16)


def make_lead(received, share, lead_tiles):
    feat = received.shape[2]
    shape = jax.ShapeDtypeStruct((TILE, feat), BF16)
    return pl.pallas_call(
        functools.partial(lead_kernel, share), out_shape=[shape] * lead_tiles, name="lead"
    )(received)


def diag_inverse(block):
    size, width = block.shape[0], 8
    count = size // width
    sub = iota((width, size), 0)
    lane = iota((width, size), 1)
    left = [block[q * width : (q + 1) * width, :] for q in range(count)]
    right = [jnp.where(lane == sub + q * width, 1.0, 0.0).astype(F32) for q in range(count)]
    out = []
    for g in range(count):
        base = g * width
        pivot_l, pivot_r = left[g], right[g]
        cols = [
            jnp.broadcast_to(pivot_l[:, base + k : base + k + 1], (width, size)) for k in range(width)
        ]
        diag = jnp.ones((width, size), F32)
        for i in range(width):
            own = jnp.broadcast_to(cols[i][i : i + 1, :], (width, size))
            diag = jnp.where(sub == i, own, diag)
            factor = jnp.where(sub > i, cols[i] / own, 0.0)
            for k in range(i + 1, width):
                cols[k] = cols[k] - factor * jnp.broadcast_to(cols[k][i : i + 1, :], (width, size))
            pivot_l = pivot_l - factor * jnp.broadcast_to(pivot_l[i : i + 1, :], (width, size))
            pivot_r = pivot_r - factor * jnp.broadcast_to(pivot_r[i : i + 1, :], (width, size))
        scale = lax.rsqrt(diag)
        pivot_l, pivot_r = pivot_l * scale, pivot_r * scale
        out.append(pivot_r)
        if g + 1 < count:
            turned = pivot_l.T
            for q in range(g + 1, count):
                rest_l, rest_r = left[q], right[q]
                for i in range(width):
                    c = jnp.broadcast_to(turned[q * width : (q + 1) * width, i : i + 1], (width, size))
                    rest_l = rest_l - c * jnp.broadcast_to(pivot_l[i : i + 1, :], (width, size))
                    rest_r = rest_r - c * jnp.broadcast_to(pivot_r[i : i + 1, :], (width, size))
                left[q], right[q] = rest_l, rest_r
    return jnp.concatenate(out, axis=0)


def chol_kernel(cols_ref, out_ref, work_ref, high_ref, low_ref):
    blocks = PANEL // TILE
    feats = cols_ref[...]
    half = half_norms(feats)
    half_row = as_row(half)
    eye = iota((TILE, PANEL), 0) - iota((TILE, PANEL), 1)
    for k in range(blocks):
        rows = slice(k * TILE, (k + 1) * TILE)
        block = rbf(feats[rows], half[rows], feats, half_row)
        work_ref[rows, :] = block + jnp.where(eye == -k * TILE, noise_var, 0.0)
    lane = iota((TILE, PANEL), 1)

    def step(k, carry):
        base = pl.multiple_of(k * TILE, TILE)
        inverse = diag_inverse(work_ref[pl.ds(base, TILE), pl.ds(base, TILE)])
        work_ref[pl.ds(base, TILE), pl.ds(base, TILE)] = jnp.where(
            iota((TILE, TILE), 0) == iota((TILE, TILE), 1), 1.0, 0.0
        )
        row = dot_split(split(inverse), split(work_ref[pl.ds(base, TILE), :]))
        out_ref[pl.ds(base, TILE), :] = jnp.where(lane < base + TILE, row, 0.0)
        high, low = split(row)
        high_ref[...] = high
        low_ref[...] = low

        def trail(i, inner):
            start = pl.multiple_of(i * TILE, TILE)
            work_ref[pl.ds(start, TILE), pl.ds(base, TILE)] = jnp.zeros((TILE, TILE), F32)
            lower = (high_ref[:, pl.ds(start, TILE)], low_ref[:, pl.ds(start, TILE)])
            work_ref[pl.ds(start, TILE), :] -= dot_split(lower, (high_ref[...], low_ref[...]), TN)
            return inner

        lax.fori_loop(k + 1, blocks, trail, 0)
        return carry

    lax.fori_loop(0, blocks, step, 0)


def make_inverse(columns):
    return pl.pallas_call(
        chol_kernel,
        out_shape=jax.ShapeDtypeStruct((PANEL, PANEL), F32),
        scratch_shapes=[
            pltpu.VMEM((PANEL, PANEL), F32),
            pltpu.VMEM((TILE, PANEL), BF16),
            pltpu.VMEM((TILE, PANEL), BF16),
        ],
        compiler_params=pltpu.CompilerParams(vmem_limit_bytes=40 << 20),
        name="cholesky",
    )(columns)


def panel_kernel(
    share, row_count, col_count, rows_blk, place_ref, recv_ref, cols_ref, next_ref, inv_ref,
    panel_ref, update_ref, feats_ref, slots_ref, high_ref, low_ref, half_ref, own_ref, own_half_ref,
):
    step = pl.program_id(0)
    row_index, col_index = place_ref[0], place_ref[1]
    col_tiles = PANEL // TILE // col_count
    width = col_tiles * TILE
    parts, per_part = recv_ref.shape[0], recv_ref.shape[1]
    groups = per_part * share // TILE
    total = parts * groups

    @pl.when(step == 0)
    def _():
        for p in range(parts):
            for g in range(groups):
                q = p * groups + g
                slots_ref[:, q * TILE : (q + 1) * TILE] = jnp.broadcast_to(
                    read_slots(recv_ref, (p,), share, g), (8, TILE)
                )
                feats_ref[q * TILE : (q + 1) * TILE, :] = gather_rows(recv_ref, (p,), share, g)
        half_row = as_row(half_norms(cols_ref[...]))
        half_ref[...] = jnp.broadcast_to(half_row, (8, PANEL))
        inverse = split(inv_ref[...])
        own = []
        for t in range(col_tiles):
            start = pl.multiple_of((t * col_count + col_index) * TILE, TILE)
            own_ref[t * TILE : (t + 1) * TILE, :] = next_ref[pl.ds(start, TILE), :]
            own.append(inv_ref[pl.ds(start, TILE), :])
        own_feats = own_ref[...]
        own_half = half_norms(own_feats)
        own_half_ref[...] = jnp.broadcast_to(as_row(own_half), (8, width))
        cross = rbf(own_feats, own_half, cols_ref[...], half_row)
        solved = dot_split(split(dot_split(split(cross), inverse, NT)), inverse)
        right = jnp.concatenate(own + [solved], axis=0)
        high, low = split(right.T)
        high_ref[...] = high
        low_ref[...] = low

    def body(diagonal):
        slot = iota((rows_blk, TILE), 0) + step * rows_blk
        pick = jnp.concatenate(
            [one_hot(slot == slots_ref[0:1, q * TILE : (q + 1) * TILE]) for q in range(total)], axis=1
        )
        feats = dot(pick, feats_ref[...]).astype(BF16)
        half = half_norms(feats)
        kern = rbf(feats, half, cols_ref[...], half_ref[0:1, :])
        kern_next = rbf(feats, half, own_ref[...], own_half_ref[0:1, :])
        if diagonal:
            local = iota((rows_blk, 1), 0) + step * rows_blk
            place = (local // TILE * row_count + row_index) * TILE + local % TILE
            kern = kern + jnp.where(place == iota((rows_blk, PANEL), 1), noise_var, 0.0)
            index = iota((rows_blk, width), 1)
            column = PANEL + (index // TILE * col_count + col_index) * TILE + index % TILE
            kern_next = kern_next + jnp.where(place == column, noise_var, 0.0)
        result = dot_split(split(kern), (high_ref[...], low_ref[...]))
        update = kern_next - result[:, width:]
        for t in range(col_tiles):
            where = pl.ds(t, rows_blk, stride=col_tiles) if col_tiles > 1 else slice(None)
            panel_ref[where, :] = result[:, t * TILE : (t + 1) * TILE]
            update_ref[where, :] = update[:, t * TILE : (t + 1) * TILE]

    lead_rows = max(2 * PANEL // row_count, TILE)
    has_diag = step * rows_blk < lead_rows

    @pl.when(has_diag)
    def _():
        body(True)

    @pl.when(jnp.logical_not(has_diag))
    def _():
        body(False)


def make_outputs(received, columns, following, inverse, share, row_count, col_count):
    parts, per_part, _, feat = received.shape
    local_rows = parts * per_part * share
    col_tiles = PANEL // TILE // col_count
    width = col_tiles * TILE
    rows_blk = 256
    row_index = lax.axis_index("row")
    col_index = lax.axis_index("col")
    place = jnp.stack([row_index, col_index]).astype(jnp.int32)
    whole = lambda *shape: pl.BlockSpec(shape, lambda i, s: (0,) * len(shape), pipeline_mode=pl.Buffered(1))
    out = jax.ShapeDtypeStruct((local_rows * col_tiles, TILE), F32)
    out_spec = pl.BlockSpec((rows_blk * col_tiles, TILE), lambda i, s: (i, 0))
    return pl.pallas_call(
        functools.partial(panel_kernel, share, row_count, col_count, rows_blk),
        out_shape=[out, out],
        grid_spec=pltpu.PrefetchScalarGridSpec(
            num_scalar_prefetch=1,
            grid=(local_rows // rows_blk,),
            in_specs=[
                whole(*received.shape),
                whole(PANEL, feat),
                whole(*following.shape),
                whole(PANEL, PANEL),
            ],
            out_specs=[out_spec, out_spec],
            scratch_shapes=[
                pltpu.VMEM((local_rows, feat), BF16),
                pltpu.VMEM((8, local_rows), jnp.int32),
                pltpu.VMEM((PANEL, 2 * width), BF16),
                pltpu.VMEM((PANEL, 2 * width), BF16),
                pltpu.VMEM((8, PANEL), F32),
                pltpu.VMEM((width, feat), BF16),
                pltpu.VMEM((8, width), F32),
            ],
        ),
        compiler_params=pltpu.CompilerParams(vmem_limit_bytes=56 << 20),
        name="panels",
    )(place, received, columns, following, inverse)


def shift(value, axis, distance, size):
    return lax.ppermute(value, axis, [(i, (i + distance) % size) for i in range(size)])


def sum_over(value, axis, size):
    step = 1
    while step < size:
        value = value + lax.ppermute(value, axis, [(i, i ^ step) for i in range(size)])
        step *= 2
    return value


def per_device(images, weight_in, bias_in, weight_out, feature_scale, position):
    image_rows = images.shape[0]
    feat = weight_out.shape[1]
    row_count = lax.axis_size("row")
    col_count = lax.axis_size("col")
    share = image_rows // row_count
    lead_tiles = 2 * PANEL // (TILE * row_count)
    bucket = make_features(
        images, weight_in, bias_in, weight_out, feature_scale, position, row_count
    )
    received = lax.all_to_all(bucket, "row", split_axis=0, concat_axis=0, tiled=True)
    lead = make_lead(received, share, lead_tiles)
    columns = lax.all_gather(sum_over(lead[0], "col", col_count), "row", axis=0, tiled=True)
    received, columns, rest = lax.optimization_barrier((received, columns, lead[1:]))
    others = [shift(received, "col", d, col_count) for d in range(1, col_count)]
    every = jnp.stack([received] + others, axis=0)
    for tile in rest:
        more = lax.all_gather(sum_over(tile, "col", col_count), "row", axis=0, tiled=True)
        columns = jnp.concatenate([columns, more], axis=0)
    first, following = columns[:PANEL], columns[PANEL:]
    inverse = make_inverse(first)
    panel, update = make_outputs(every, first, following, inverse, share, row_count, col_count)
    shape_out = (image_rows * col_count // TILE, TILE, PANEL // TILE // col_count, TILE)
    return panel.reshape(shape_out), update.reshape(shape_out)


def solution(mesh):
    in_specs = (P(("row", "col"), None), P(), P(), P(), P(), P(("row", "col")))
    out_specs = (P(None, "row", None, "col"), P(None, "row", None, "col"))
    return jax.shard_map(
        per_device, mesh=mesh, in_specs=in_specs, out_specs=out_specs, check_vma=False
    )
```

```python
import functools

import jax
import jax.numpy as jnp
from jax import lax
from jax.experimental import pallas as pl
from jax.experimental.pallas import tpu as pltpu
from jax.sharding import PartitionSpec as P

TILE = 128
PANEL = 1024
META = 16
F32 = jnp.float32
BF16 = jnp.bfloat16
NN = (((1,), (0,)), ((), ()))
NT = (((1,), (1,)), ((), ()))
TN = (((0,), (0,)), ((), ()))

noise_var = 0.5


def iota(shape, dim):
    return lax.broadcasted_iota(jnp.int32, shape, dim)


def one_hot(cond):
    return jnp.where(cond, 1.0, 0.0).astype(BF16)


def dot(left, right, dims=NN):
    return lax.dot_general(left, right, dims, preferred_element_type=F32)


def split(value):
    high = value.astype(BF16)
    return high, (value - high.astype(F32)).astype(BF16)


def dot_split(left, right, dims=NN):
    return dot(left[0], right[0], dims) + (
        dot(left[0], right[1], dims) + dot(left[1], right[0], dims)
    )


def half_norms(feats):
    wide = feats.astype(F32)
    return 0.5 * jnp.sum(wide * wide, axis=1, keepdims=True)


def as_row(column):
    rows = column.shape[0]
    return jnp.broadcast_to(column, (rows, TILE)).T[:1, :]


def rbf(left, left_half, right, right_half_row):
    cross = dot(left, right, NT)
    return jnp.exp(jnp.minimum(cross - left_half - right_half_row, 0.0))


def feature_kernel(
    share, row_count, pos_ref, img_ref, win_ref, bias_ref, wout_ref, scale_ref, out_ref, acc_ref
):
    step = pl.program_id(0)
    preact = dot(img_ref[...], win_ref[...]) + bias_ref[...]
    hidden = 0.5 * preact * (1.0 + jnp.tanh(0.7978845608 * (preact + 0.044715 * preact * preact * preact)))
    part = dot(hidden.astype(BF16), wout_ref[...])

    @pl.when(step == 0)
    def _():
        acc_ref[...] = part

    @pl.when(step > 0)
    def _():
        acc_ref[...] += part

    @pl.when(step == pl.num_programs(0) - 1)
    def _():
        images = row_count * share
        feats = (acc_ref[...] * scale_ref[...]).astype(BF16)
        place = pos_ref[...]
        tile = place // TILE
        group = tile % row_count
        member = iota((row_count, images), 0) == group
        before = one_hot(iota((images, images), 0) < iota((images, images), 1))
        rank = dot(one_hot(member), before)
        target = jnp.where(member, rank + (share * iota((row_count, images), 0)).astype(F32), 0.0)
        target = jnp.sum(target, axis=0, keepdims=True).astype(jnp.int32)
        order = one_hot(iota((images, images), 0) == target)
        sorted_feats = dot(order, feats).astype(BF16)
        meta_row = iota((META, images), 0)
        meta = jnp.where(meta_row == 0, tile // row_count, jnp.where(meta_row == 1, place % TILE, 0))
        meta = meta.astype(F32).astype(BF16)
        lane = iota((TILE, images), 0) % share
        for r in range(row_count):
            out_ref[r, :share, :] = sorted_feats[r * share : (r + 1) * share, :]
            sel = one_hot(lane + r * share == target)
            spread = dot(meta, sel, NT).astype(BF16)
            out_ref[r, share:, :TILE] = spread
            out_ref[r, share:, TILE:] = jnp.zeros((META, out_ref.shape[2] - TILE), BF16)


def make_features(images, weight_in, bias_in, weight_out, feature_scale, position, row_count):
    rows, din = images.shape
    hid, feat = weight_out.shape
    share = rows // row_count
    block = 512
    operands = (
        position.reshape(1, rows),
        images,
        weight_in,
        bias_in.reshape(1, hid),
        weight_out,
        feature_scale.reshape(1, feat),
    )
    return pl.pallas_call(
        functools.partial(feature_kernel, share, row_count),
        out_shape=jax.ShapeDtypeStruct((row_count, share + META, feat), BF16),
        grid=(hid // block,),
        in_specs=[
            pl.BlockSpec((1, rows), lambda i: (0, 0)),
            pl.BlockSpec((rows, din), lambda i: (0, 0)),
            pl.BlockSpec((din, block), lambda i: (0, i)),
            pl.BlockSpec((1, block), lambda i: (0, i)),
            pl.BlockSpec((block, feat), lambda i: (i, 0)),
            pl.BlockSpec((1, feat), lambda i: (0, 0)),
        ],
        out_specs=pl.BlockSpec((row_count, share + META, feat), lambda i: (0, 0, 0)),
        scratch_shapes=[pltpu.VMEM((rows, feat), F32)],
        compiler_params=pltpu.CompilerParams(vmem_limit_bytes=32 << 20),
        name="features",
    )(*[pltpu.with_memory_space_constraint(x, pltpu.HBM) for x in operands])


def read_slots(block_ref, lead, share, group):
    per = TILE // share
    lane = iota((META, TILE), 1) // share
    meta = None
    for j in range(per):
        piece = block_ref[lead + (group * per + j, slice(share, share + META), slice(0, TILE))].astype(F32)
        meta = piece if meta is None else jnp.where(lane == j, piece, meta)
    return (meta[0:1, :] * TILE + meta[1:2, :]).astype(jnp.int32)


def gather_rows(block_ref, lead, share, group):
    per = TILE // share
    return jnp.concatenate(
        [block_ref[lead + (group * per + j, slice(0, share), slice(None))] for j in range(per)], axis=0
    )


def lead_kernel(share, recv_ref, *out_refs):
    groups = recv_ref.shape[0] * share // TILE
    slots = [read_slots(recv_ref, (), share, g) for g in range(groups)]
    rows = jnp.concatenate([gather_rows(recv_ref, (), share, g) for g in range(groups)], axis=0)
    for t, out_ref in enumerate(out_refs):
        pick = jnp.concatenate(
            [one_hot(iota((TILE, TILE), 0) + t * TILE == s) for s in slots], axis=1
        )
        out_ref[...] = dot(pick, rows).astype(BF16)


def make_lead(received, share, lead_tiles):
    feat = received.shape[2]
    shape = jax.ShapeDtypeStruct((TILE, feat), BF16)
    return pl.pallas_call(
        functools.partial(lead_kernel, share), out_shape=[shape] * lead_tiles, name="lead"
    )(received)


def diag_inverse(block):
    size, width = block.shape[0], 8
    count = size // width
    sub = iota((width, size), 0)
    lane = iota((width, size), 1)
    left = [block[q * width : (q + 1) * width, :] for q in range(count)]
    right = [jnp.where(lane == sub + q * width, 1.0, 0.0).astype(F32) for q in range(count)]
    out = []
    for g in range(count):
        base = g * width
        pivot_l, pivot_r = left[g], right[g]
        cols = [
            jnp.broadcast_to(pivot_l[:, base + k : base + k + 1], (width, size)) for k in range(width)
        ]
        diag = jnp.ones((width, size), F32)
        for i in range(width):
            own = jnp.broadcast_to(cols[i][i : i + 1, :], (width, size))
            diag = jnp.where(sub == i, own, diag)
            factor = jnp.where(sub > i, cols[i] / own, 0.0)
            for k in range(i + 1, width):
                cols[k] = cols[k] - factor * jnp.broadcast_to(cols[k][i : i + 1, :], (width, size))
            pivot_l = pivot_l - factor * jnp.broadcast_to(pivot_l[i : i + 1, :], (width, size))
            pivot_r = pivot_r - factor * jnp.broadcast_to(pivot_r[i : i + 1, :], (width, size))
        scale = lax.rsqrt(diag)
        pivot_l, pivot_r = pivot_l * scale, pivot_r * scale
        out.append(pivot_r)
        if g + 1 < count:
            turned = pivot_l.T
            for q in range(g + 1, count):
                rest_l, rest_r = left[q], right[q]
                for i in range(width):
                    c = jnp.broadcast_to(turned[q * width : (q + 1) * width, i : i + 1], (width, size))
                    rest_l = rest_l - c * jnp.broadcast_to(pivot_l[i : i + 1, :], (width, size))
                    rest_r = rest_r - c * jnp.broadcast_to(pivot_r[i : i + 1, :], (width, size))
                left[q], right[q] = rest_l, rest_r
    return jnp.concatenate(out, axis=0)


def chol_kernel(cols_ref, out_ref, work_ref, high_ref, low_ref):
    blocks = PANEL // TILE
    feats = cols_ref[...]
    half = half_norms(feats)
    half_row = as_row(half)
    eye = iota((TILE, PANEL), 0) - iota((TILE, PANEL), 1)
    for k in range(blocks):
        rows = slice(k * TILE, (k + 1) * TILE)
        block = rbf(feats[rows], half[rows], feats, half_row)
        work_ref[rows, :] = block + jnp.where(eye == -k * TILE, noise_var, 0.0)
    lane = iota((TILE, PANEL), 1)

    def step(k, carry):
        base = pl.multiple_of(k * TILE, TILE)
        inverse = diag_inverse(work_ref[pl.ds(base, TILE), pl.ds(base, TILE)])
        work_ref[pl.ds(base, TILE), pl.ds(base, TILE)] = jnp.where(
            iota((TILE, TILE), 0) == iota((TILE, TILE), 1), 1.0, 0.0
        )
        row = dot_split(split(inverse), split(work_ref[pl.ds(base, TILE), :]))
        out_ref[pl.ds(base, TILE), :] = jnp.where(lane < base + TILE, row, 0.0)
        high, low = split(row)
        high_ref[...] = high
        low_ref[...] = low

        def trail(i, inner):
            start = pl.multiple_of(i * TILE, TILE)
            work_ref[pl.ds(start, TILE), pl.ds(base, TILE)] = jnp.zeros((TILE, TILE), F32)
            lower = (high_ref[:, pl.ds(start, TILE)], low_ref[:, pl.ds(start, TILE)])
            work_ref[pl.ds(start, TILE), :] -= dot_split(lower, (high_ref[...], low_ref[...]), TN)
            return inner

        lax.fori_loop(k + 1, blocks, trail, 0)
        return carry

    lax.fori_loop(0, blocks, step, 0)


def make_inverse(columns):
    return pl.pallas_call(
        chol_kernel,
        out_shape=jax.ShapeDtypeStruct((PANEL, PANEL), F32),
        scratch_shapes=[
            pltpu.VMEM((PANEL, PANEL), F32),
            pltpu.VMEM((TILE, PANEL), BF16),
            pltpu.VMEM((TILE, PANEL), BF16),
        ],
        compiler_params=pltpu.CompilerParams(vmem_limit_bytes=24 << 20),
        cost_estimate=pl.CostEstimate(flops=40 * 10**9, transcendentals=1 << 20, bytes_accessed=5 << 20),
        name="cholesky",
    )(columns)


def panel_kernel(share, row_count, col_count, rows_blk, parts, pieces, place_ref, *refs):
    recv_refs, next_refs = refs[:parts], refs[parts : parts + pieces]
    (cols_ref, inv_ref, panel_ref, update_ref, feats_ref, slots_ref, high_ref, low_ref, half_ref,
     own_ref, own_half_ref) = refs[parts + pieces :]
    step = pl.program_id(0)
    row_index, col_index = place_ref[0], place_ref[1]
    col_tiles = PANEL // TILE // col_count
    width = col_tiles * TILE
    groups = recv_refs[0].shape[0] * share // TILE
    total = parts * groups

    @pl.when(step == 0)
    def _():
        for p in range(parts):
            for g in range(groups):
                q = p * groups + g
                slots_ref[:, q * TILE : (q + 1) * TILE] = jnp.broadcast_to(
                    read_slots(recv_refs[p], (), share, g), (8, TILE)
                )
                feats_ref[q * TILE : (q + 1) * TILE, :] = gather_rows(recv_refs[p], (), share, g)
        half_row = as_row(half_norms(cols_ref[...]))
        half_ref[...] = jnp.broadcast_to(half_row, (8, PANEL))
        inverse = split(inv_ref[...])
        own = []
        for t in range(col_tiles):
            tile = t * col_count + col_index
            for n, next_ref in enumerate(next_refs):

                @pl.when(place_ref[2 + n] == tile)
                def _():
                    own_ref[t * TILE : (t + 1) * TILE, :] = next_ref[...]

            own.append(inv_ref[pl.ds(pl.multiple_of(tile * TILE, TILE), TILE), :])
        own_feats = own_ref[...]
        own_half = half_norms(own_feats)
        own_half_ref[...] = jnp.broadcast_to(as_row(own_half), (8, width))
        cross = rbf(own_feats, own_half, cols_ref[...], half_row)
        solved = dot_split(split(dot_split(split(cross), inverse, NT)), inverse)
        right = jnp.concatenate(own + [solved], axis=0)
        high, low = split(right.T)
        high_ref[...] = high
        low_ref[...] = low

    def body(diagonal):
        slot = iota((rows_blk, TILE), 0) + step * rows_blk
        pick = jnp.concatenate(
            [one_hot(slot == slots_ref[0:1, q * TILE : (q + 1) * TILE]) for q in range(total)], axis=1
        )
        feats = dot(pick, feats_ref[...]).astype(BF16)
        half = half_norms(feats)
        kern = rbf(feats, half, cols_ref[...], half_ref[0:1, :])
        kern_next = rbf(feats, half, own_ref[...], own_half_ref[0:1, :])
        if diagonal:
            local = iota((rows_blk, 1), 0) + step * rows_blk
            place = (local // TILE * row_count + row_index) * TILE + local % TILE
            kern = kern + jnp.where(place == iota((rows_blk, PANEL), 1), noise_var, 0.0)
            index = iota((rows_blk, width), 1)
            column = PANEL + (index // TILE * col_count + col_index) * TILE + index % TILE
            kern_next = kern_next + jnp.where(place == column, noise_var, 0.0)
        result = dot_split(split(kern), (high_ref[...], low_ref[...]))
        update = kern_next - result[:, width:]
        for t in range(col_tiles):
            where = pl.ds(t, rows_blk, stride=col_tiles) if col_tiles > 1 else slice(None)
            panel_ref[where, :] = result[:, t * TILE : (t + 1) * TILE]
            update_ref[where, :] = update[:, t * TILE : (t + 1) * TILE]

    lead_rows = max(2 * PANEL // row_count, TILE)
    has_diag = step * rows_blk < lead_rows

    @pl.when(has_diag)
    def _():
        body(True)

    @pl.when(jnp.logical_not(has_diag))
    def _():
        body(False)


def make_outputs(parts, pieces, piece_tiles, columns, inverse, share, row_count, col_count):
    feat = columns.shape[1]
    local_rows = len(parts) * parts[0].shape[0] * share
    col_tiles = PANEL // TILE // col_count
    width = col_tiles * TILE
    rows_blk = 256
    place = jnp.stack([lax.axis_index("row"), lax.axis_index("col")] + piece_tiles).astype(jnp.int32)
    operands = (*parts, *pieces, columns, inverse)
    out = jax.ShapeDtypeStruct((local_rows * col_tiles, TILE), F32)
    out_spec = pl.BlockSpec((rows_blk * col_tiles, TILE), lambda i, s: (i, 0))
    return pl.pallas_call(
        functools.partial(panel_kernel, share, row_count, col_count, rows_blk, len(parts), len(pieces)),
        out_shape=[out, out],
        grid_spec=pltpu.PrefetchScalarGridSpec(
            num_scalar_prefetch=1,
            grid=(local_rows // rows_blk,),
            in_specs=[pl.BlockSpec(memory_space=pltpu.VMEM)] * len(operands),
            out_specs=[out_spec, out_spec],
            scratch_shapes=[
                pltpu.VMEM((local_rows, feat), BF16),
                pltpu.VMEM((8, local_rows), jnp.int32),
                pltpu.VMEM((PANEL, 2 * width), BF16),
                pltpu.VMEM((PANEL, 2 * width), BF16),
                pltpu.VMEM((8, PANEL), F32),
                pltpu.VMEM((width, feat), BF16),
                pltpu.VMEM((8, width), F32),
            ],
        ),
        compiler_params=pltpu.CompilerParams(vmem_limit_bytes=36 << 20),
        name="panels",
    )(place, *operands)


def shift(value, axis, distance, size):
    return lax.ppermute(value, axis, [(i, (i + distance) % size) for i in range(size)])


def exchange(value, axis, step, size):
    return lax.ppermute(value, axis, [(i, i ^ step) for i in range(size)])


def sum_over(value, axis, size):
    step = 1
    while step < size:
        value = value + exchange(value, axis, step, size)
        step *= 2
    return value


def next_tiles(tile, row_count, col_count):
    turns = PANEL // TILE // col_count
    row_index, col_index = lax.axis_index("row"), lax.axis_index("col")
    pieces, piece_tiles = [], []
    for turn in range(turns):
        pairs = []
        for r in range(row_count):
            for c in range(col_count):
                owner = c + col_count * ((r // col_count + turn) % turns)
                pairs.append((owner * col_count + r % col_count, r * col_count + c))
        pieces.append(lax.ppermute(tile, ("row", "col"), pairs))
        piece_tiles.append(col_index + col_count * ((row_index // col_count + turn) % turns))
    return pieces, piece_tiles


def per_device(images, weight_in, bias_in, weight_out, feature_scale, position):
    image_rows = images.shape[0]
    feat = weight_out.shape[1]
    row_count = lax.axis_size("row")
    col_count = lax.axis_size("col")
    share = image_rows // row_count
    lead_tiles = 2 * PANEL // (TILE * row_count)
    bucket = make_features(
        images, weight_in, bias_in, weight_out, feature_scale, position, row_count
    )
    received = lax.all_to_all(bucket, "row", split_axis=0, concat_axis=0, tiled=True)
    lead = make_lead(received, share, lead_tiles)
    first, rest = lax.optimization_barrier((sum_over(lead[0], "col", col_count), lead[1:]))
    rest = [[tile] + [shift(tile, "col", d, col_count) for d in range(1, col_count)] for tile in rest]
    columns = lax.all_gather(first, "row", axis=0, tiled=True)
    rest = [sum(pieces[1:], pieces[0]) for pieces in rest]
    columns, rest, received = lax.optimization_barrier((columns, rest, received))
    if rest:
        pieces, piece_tiles = next_tiles(rest[0], row_count, col_count)
    else:
        pieces = [columns[PANEL + t * TILE : PANEL + (t + 1) * TILE] for t in range(PANEL // TILE)]
        piece_tiles = [jnp.int32(t) for t in range(PANEL // TILE)]
    parts = [received] + [shift(received, "col", d, col_count) for d in range(1, col_count)]
    inverse = make_inverse(columns[:PANEL])
    panel, update = make_outputs(
        parts, pieces, piece_tiles, columns[:PANEL], inverse, share, row_count, col_count
    )
    shape_out = (image_rows * col_count // TILE, TILE, PANEL // TILE // col_count, TILE)
    return panel.reshape(shape_out), update.reshape(shape_out)


def solution(mesh):
    in_specs = (P(("row", "col"), None), P(), P(), P(), P(), P(("row", "col")))
    out_specs = (P(None, "row", None, "col"), P(None, "row", None, "col"))
    return jax.shard_map(
        per_device, mesh=mesh, in_specs=in_specs, out_specs=out_specs, check_vma=False
    )
```

```python
import functools

import jax
import jax.numpy as jnp
from jax import lax
from jax.experimental import pallas as pl
from jax.experimental.pallas import tpu as pltpu
from jax.sharding import PartitionSpec as P

TILE = 128
PANEL = 1024
META = 16
F32 = jnp.float32
BF16 = jnp.bfloat16
NN = (((1,), (0,)), ((), ()))
NT = (((1,), (1,)), ((), ()))
TN = (((0,), (0,)), ((), ()))

noise_var = 0.5


def iota(shape, dim):
    return lax.broadcasted_iota(jnp.int32, shape, dim)


def one_hot(cond):
    return jnp.where(cond, 1.0, 0.0).astype(BF16)


def dot(left, right, dims=NN):
    return lax.dot_general(left, right, dims, preferred_element_type=F32)


def split(value):
    high = value.astype(BF16)
    return high, (value - high.astype(F32)).astype(BF16)


def dot_split(left, right, dims=NN):
    return dot(left[0], right[0], dims) + (
        dot(left[0], right[1], dims) + dot(left[1], right[0], dims)
    )


def half_norms(feats):
    wide = feats.astype(F32)
    return 0.5 * jnp.sum(wide * wide, axis=1, keepdims=True)


def as_row(column):
    rows = column.shape[0]
    return jnp.broadcast_to(column, (rows, TILE)).T[:1, :]


def rbf(left, left_half, right, right_half_row):
    cross = dot(left, right, NT)
    return jnp.exp(jnp.minimum(cross - left_half - right_half_row, 0.0))


def feature_kernel(
    share, row_count, pos_ref, img_ref, win_ref, bias_ref, wout_ref, scale_ref, out_ref, acc_ref
):
    step = pl.program_id(0)
    preact = dot(img_ref[...], win_ref[...]) + bias_ref[...]
    hidden = 0.5 * preact * (1.0 + jnp.tanh(0.7978845608 * (preact + 0.044715 * preact * preact * preact)))
    part = dot(hidden.astype(BF16), wout_ref[...])

    @pl.when(step == 0)
    def _():
        acc_ref[...] = part

    @pl.when(step > 0)
    def _():
        acc_ref[...] += part

    @pl.when(step == pl.num_programs(0) - 1)
    def _():
        images = row_count * share
        feats = (acc_ref[...] * scale_ref[...]).astype(BF16)
        place = pos_ref[...]
        tile = place // TILE
        group = tile % row_count
        member = iota((row_count, images), 0) == group
        before = one_hot(iota((images, images), 0) < iota((images, images), 1))
        rank = dot(one_hot(member), before)
        target = jnp.where(member, rank + (share * iota((row_count, images), 0)).astype(F32), 0.0)
        target = jnp.sum(target, axis=0, keepdims=True).astype(jnp.int32)
        order = one_hot(iota((images, images), 0) == target)
        sorted_feats = dot(order, feats).astype(BF16)
        meta_row = iota((META, images), 0)
        meta = jnp.where(meta_row == 0, tile // row_count, jnp.where(meta_row == 1, place % TILE, 0))
        meta = meta.astype(F32).astype(BF16)
        lane = iota((TILE, images), 0) % share
        for r in range(row_count):
            out_ref[r, :share, :] = sorted_feats[r * share : (r + 1) * share, :]
            sel = one_hot(lane + r * share == target)
            spread = dot(meta, sel, NT).astype(BF16)
            out_ref[r, share:, :TILE] = spread
            out_ref[r, share:, TILE:] = jnp.zeros((META, out_ref.shape[2] - TILE), BF16)


def make_features(images, weight_in, bias_in, weight_out, feature_scale, position, row_count):
    rows, din = images.shape
    hid, feat = weight_out.shape
    share = rows // row_count
    block = 512
    operands = (
        position.reshape(1, rows),
        images,
        weight_in,
        bias_in.reshape(1, hid),
        weight_out,
        feature_scale.reshape(1, feat),
    )
    return pl.pallas_call(
        functools.partial(feature_kernel, share, row_count),
        out_shape=jax.ShapeDtypeStruct((row_count, share + META, feat), BF16),
        grid=(hid // block,),
        in_specs=[
            pl.BlockSpec((1, rows), lambda i: (0, 0)),
            pl.BlockSpec((rows, din), lambda i: (0, 0)),
            pl.BlockSpec((din, block), lambda i: (0, i)),
            pl.BlockSpec((1, block), lambda i: (0, i)),
            pl.BlockSpec((block, feat), lambda i: (i, 0)),
            pl.BlockSpec((1, feat), lambda i: (0, 0)),
        ],
        out_specs=pl.BlockSpec((row_count, share + META, feat), lambda i: (0, 0, 0)),
        scratch_shapes=[pltpu.VMEM((rows, feat), F32)],
        compiler_params=pltpu.CompilerParams(vmem_limit_bytes=32 << 20),
        name="features",
    )(*[pltpu.with_memory_space_constraint(x, pltpu.HBM) for x in operands])


def read_slots(block_ref, lead, share, group):
    per = TILE // share
    lane = iota((META, TILE), 1) // share
    meta = None
    for j in range(per):
        piece = block_ref[lead + (group * per + j, slice(share, share + META), slice(0, TILE))].astype(F32)
        meta = piece if meta is None else jnp.where(lane == j, piece, meta)
    return (meta[0:1, :] * TILE + meta[1:2, :]).astype(jnp.int32)


def gather_rows(block_ref, lead, share, group):
    per = TILE // share
    return jnp.concatenate(
        [block_ref[lead + (group * per + j, slice(0, share), slice(None))] for j in range(per)], axis=0
    )


def lead_kernel(share, recv_ref, *out_refs):
    groups = recv_ref.shape[0] * share // TILE
    slots = [read_slots(recv_ref, (), share, g) for g in range(groups)]
    rows = jnp.concatenate([gather_rows(recv_ref, (), share, g) for g in range(groups)], axis=0)
    for t, out_ref in enumerate(out_refs):
        pick = jnp.concatenate(
            [one_hot(iota((TILE, TILE), 0) + t * TILE == s) for s in slots], axis=1
        )
        out_ref[...] = dot(pick, rows).astype(BF16)


def make_lead(received, share, lead_tiles):
    feat = received.shape[2]
    shape = jax.ShapeDtypeStruct((TILE, feat), BF16)
    return pl.pallas_call(
        functools.partial(lead_kernel, share), out_shape=[shape] * lead_tiles, name="lead"
    )(received)


def diag_inverse(block):
    size, width, ahead = block.shape[0], 8, 2
    count = size // width
    shape = (width, size)
    sub, lane = iota(shape, 0), iota(shape, 1)
    spread = lambda x: jnp.broadcast_to(x, shape)
    left = [block[q * width : (q + 1) * width, :] for q in range(count)]
    right = [jnp.where(lane == sub + q * width, 1.0, 0.0).astype(F32) for q in range(count)]
    columns = {}
    out = []
    for g in range(count):
        rows = range(g, min(g + ahead + 1, count))
        for q in rows:
            for h in range(g, min(q, g + ahead - 1) + 1):
                if (q, h) not in columns:
                    columns[q, h] = [spread(left[q][:, h * width + k : h * width + k + 1]) for k in range(width)]
        diag = jnp.ones(shape, F32)
        for i in range(width):
            own = spread(columns[g, g][i][i : i + 1, :])
            inv = 1.0 / own
            diag = jnp.where(sub == i, own, diag)
            source = {q: columns[q, g][i] for q in rows}
            factor = {q: source[q] * inv for q in rows}
            factor[g] = jnp.where(sub > i, factor[g], 0.0)
            for h in range(g, min(g + ahead, count)):
                for k in range(i + 1 if h == g else 0, width):
                    value = spread(source[h][k : k + 1, :])
                    for q in rows:
                        if q >= h:
                            columns[q, h][k] = columns[q, h][k] - factor[q] * value
            pivot_l, pivot_r = spread(left[g][i : i + 1, :]), spread(right[g][i : i + 1, :])
            for q in rows:
                left[q] = left[q] - factor[q] * pivot_l
                right[q] = right[q] - factor[q] * pivot_r
        scale = lax.rsqrt(diag)
        pivot_l, pivot_r = left[g] * scale, right[g] * scale
        out.append(pivot_r)
        first = g + ahead + 1
        if first < count:
            high = [x.astype(BF16).astype(F32) for x in (pivot_l, pivot_r)]
            low = [x - h for x, h in zip((pivot_l, pivot_r), high)]
            zero = jnp.zeros_like(pivot_l)
            lhs = jnp.concatenate([high[0], high[0], low[0], zero], axis=0).astype(BF16)
            high, low = jnp.concatenate(high, axis=1), jnp.concatenate(low, axis=1)
            rhs = jnp.concatenate([high, low, high, jnp.zeros_like(high)], axis=0).astype(BF16)
            gone = dot(lhs, rhs, TN)
            for q in range(first, count):
                left[q] = left[q] - gone[q * width : (q + 1) * width, :size]
                right[q] = right[q] - gone[q * width : (q + 1) * width, size:]
    return jnp.concatenate(out, axis=0)


def chol_kernel(cols_ref, out_ref, work_ref, high_ref, low_ref):
    blocks = PANEL // TILE
    feats = cols_ref[...]
    half = half_norms(feats)
    half_row = as_row(half)
    eye = iota((TILE, PANEL), 0) - iota((TILE, PANEL), 1)
    for k in range(blocks):
        rows = slice(k * TILE, (k + 1) * TILE)
        block = rbf(feats[rows], half[rows], feats, half_row)
        work_ref[rows, :] = block + jnp.where(eye == -k * TILE, noise_var, 0.0)
    lane = iota((TILE, PANEL), 1)

    def step(k, carry):
        base = pl.multiple_of(k * TILE, TILE)
        inverse = diag_inverse(work_ref[pl.ds(base, TILE), pl.ds(base, TILE)])
        work_ref[pl.ds(base, TILE), pl.ds(base, TILE)] = jnp.where(
            iota((TILE, TILE), 0) == iota((TILE, TILE), 1), 1.0, 0.0
        )
        row = dot_split(split(inverse), split(work_ref[pl.ds(base, TILE), :]))
        out_ref[pl.ds(base, TILE), :] = jnp.where(lane < base + TILE, row, 0.0)
        high, low = split(row)
        high_ref[...] = high
        low_ref[...] = low

        for done in range(1, blocks):

            @pl.when(k == done - 1)
            def _():
                rest = slice(done * TILE, PANEL)
                work_ref[rest, (done - 1) * TILE : done * TILE] = jnp.zeros((PANEL - done * TILE, TILE), F32)
                lower = (high_ref[:, rest], low_ref[:, rest])
                work_ref[rest, :] -= dot_split(lower, (high_ref[...], low_ref[...]), TN)

        return carry

    lax.fori_loop(0, blocks, step, 0)


def make_inverse(columns):
    return pl.pallas_call(
        chol_kernel,
        out_shape=jax.ShapeDtypeStruct((PANEL, PANEL), F32),
        scratch_shapes=[
            pltpu.VMEM((PANEL, PANEL), F32),
            pltpu.VMEM((TILE, PANEL), BF16),
            pltpu.VMEM((TILE, PANEL), BF16),
        ],
        compiler_params=pltpu.CompilerParams(vmem_limit_bytes=24 << 20),
        cost_estimate=pl.CostEstimate(flops=40 * 10**9, transcendentals=1 << 20, bytes_accessed=5 << 20),
        name="cholesky",
    )(columns)


def panel_kernel(share, row_count, col_count, rows_blk, parts, pieces, place_ref, *refs):
    recv_refs, next_refs = refs[:parts], refs[parts : parts + pieces]
    (cols_ref, inv_ref, panel_ref, update_ref, feats_ref, slots_ref, high_ref, low_ref, half_ref,
     own_ref, own_half_ref) = refs[parts + pieces :]
    step = pl.program_id(0)
    row_index, col_index = place_ref[0], place_ref[1]
    col_tiles = PANEL // TILE // col_count
    width = col_tiles * TILE
    groups = recv_refs[0].shape[0] * share // TILE
    total = parts * groups

    @pl.when(step == 0)
    def _():
        for p in range(parts):
            for g in range(groups):
                q = p * groups + g
                slots_ref[:, q * TILE : (q + 1) * TILE] = jnp.broadcast_to(
                    read_slots(recv_refs[p], (), share, g), (8, TILE)
                )
                feats_ref[q * TILE : (q + 1) * TILE, :] = gather_rows(recv_refs[p], (), share, g)
        half_row = as_row(half_norms(cols_ref[...]))
        half_ref[...] = jnp.broadcast_to(half_row, (8, PANEL))
        inverse = split(inv_ref[...])
        own = []
        for t in range(col_tiles):
            tile = t * col_count + col_index
            for n, next_ref in enumerate(next_refs):

                @pl.when(place_ref[2 + n] == tile)
                def _():
                    own_ref[t * TILE : (t + 1) * TILE, :] = next_ref[...]

            own.append(inv_ref[pl.ds(pl.multiple_of(tile * TILE, TILE), TILE), :])
        own_feats = own_ref[...]
        own_half = half_norms(own_feats)
        own_half_ref[...] = jnp.broadcast_to(as_row(own_half), (8, width))
        cross = rbf(own_feats, own_half, cols_ref[...], half_row)
        solved = dot_split(split(dot_split(split(cross), inverse, NT)), inverse)
        right = jnp.concatenate(own + [solved], axis=0)
        high, low = split(right.T)
        high_ref[...] = high
        low_ref[...] = low

    def body(diagonal):
        slot = iota((rows_blk, TILE), 0) + step * rows_blk
        pick = jnp.concatenate(
            [one_hot(slot == slots_ref[0:1, q * TILE : (q + 1) * TILE]) for q in range(total)], axis=1
        )
        feats = dot(pick, feats_ref[...]).astype(BF16)
        half = half_norms(feats)
        kern = rbf(feats, half, cols_ref[...], half_ref[0:1, :])
        kern_next = rbf(feats, half, own_ref[...], own_half_ref[0:1, :])
        if diagonal:
            local = iota((rows_blk, 1), 0) + step * rows_blk
            place = (local // TILE * row_count + row_index) * TILE + local % TILE
            kern = kern + jnp.where(place == iota((rows_blk, PANEL), 1), noise_var, 0.0)
            index = iota((rows_blk, width), 1)
            column = PANEL + (index // TILE * col_count + col_index) * TILE + index % TILE
            kern_next = kern_next + jnp.where(place == column, noise_var, 0.0)
        result = dot_split(split(kern), (high_ref[...], low_ref[...]))
        update = kern_next - result[:, width:]
        for t in range(col_tiles):
            where = pl.ds(t, rows_blk, stride=col_tiles) if col_tiles > 1 else slice(None)
            panel_ref[where, :] = result[:, t * TILE : (t + 1) * TILE]
            update_ref[where, :] = update[:, t * TILE : (t + 1) * TILE]

    lead_rows = max(2 * PANEL // row_count, TILE)
    has_diag = step * rows_blk < lead_rows

    @pl.when(has_diag)
    def _():
        body(True)

    @pl.when(jnp.logical_not(has_diag))
    def _():
        body(False)


def make_outputs(parts, pieces, piece_tiles, columns, inverse, share, row_count, col_count):
    feat = columns.shape[1]
    local_rows = len(parts) * parts[0].shape[0] * share
    col_tiles = PANEL // TILE // col_count
    width = col_tiles * TILE
    rows_blk = 256
    place = jnp.stack([lax.axis_index("row"), lax.axis_index("col")] + piece_tiles).astype(jnp.int32)
    operands = (*parts, *pieces, columns, inverse)
    out = jax.ShapeDtypeStruct((local_rows * col_tiles, TILE), F32)
    out_spec = pl.BlockSpec((rows_blk * col_tiles, TILE), lambda i, s: (i, 0))
    return pl.pallas_call(
        functools.partial(panel_kernel, share, row_count, col_count, rows_blk, len(parts), len(pieces)),
        out_shape=[out, out],
        grid_spec=pltpu.PrefetchScalarGridSpec(
            num_scalar_prefetch=1,
            grid=(local_rows // rows_blk,),
            in_specs=[pl.BlockSpec(memory_space=pltpu.VMEM)] * len(operands),
            out_specs=[out_spec, out_spec],
            scratch_shapes=[
                pltpu.VMEM((local_rows, feat), BF16),
                pltpu.VMEM((8, local_rows), jnp.int32),
                pltpu.VMEM((PANEL, 2 * width), BF16),
                pltpu.VMEM((PANEL, 2 * width), BF16),
                pltpu.VMEM((8, PANEL), F32),
                pltpu.VMEM((width, feat), BF16),
                pltpu.VMEM((8, width), F32),
            ],
        ),
        compiler_params=pltpu.CompilerParams(vmem_limit_bytes=36 << 20),
        name="panels",
    )(place, *operands)


def shift(value, axis, distance, size):
    return lax.ppermute(value, axis, [(i, (i + distance) % size) for i in range(size)])


def exchange(value, axis, step, size):
    return lax.ppermute(value, axis, [(i, i ^ step) for i in range(size)])


def sum_over(value, axis, size):
    step = 1
    while step < size:
        value = value + exchange(value, axis, step, size)
        step *= 2
    return value


def next_tiles(tile, row_count, col_count):
    turns = PANEL // TILE // col_count
    row_index, col_index = lax.axis_index("row"), lax.axis_index("col")
    pieces, piece_tiles = [], []
    for turn in range(turns):
        pairs = []
        for r in range(row_count):
            for c in range(col_count):
                owner = c + col_count * ((r // col_count + turn) % turns)
                pairs.append((owner * col_count + r % col_count, r * col_count + c))
        pieces.append(lax.ppermute(tile, ("row", "col"), pairs))
        piece_tiles.append(col_index + col_count * ((row_index // col_count + turn) % turns))
    return pieces, piece_tiles


def per_device(images, weight_in, bias_in, weight_out, feature_scale, position):
    image_rows = images.shape[0]
    feat = weight_out.shape[1]
    row_count = lax.axis_size("row")
    col_count = lax.axis_size("col")
    share = image_rows // row_count
    lead_tiles = 2 * PANEL // (TILE * row_count)
    bucket = make_features(
        images, weight_in, bias_in, weight_out, feature_scale, position, row_count
    )
    received = lax.all_to_all(bucket, "row", split_axis=0, concat_axis=0, tiled=True)
    lead = make_lead(received, share, lead_tiles)
    first, rest = lax.optimization_barrier((sum_over(lead[0], "col", col_count), lead[1:]))
    rest = [[tile] + [shift(tile, "col", d, col_count) for d in range(1, col_count)] for tile in rest]
    columns = lax.all_gather(first, "row", axis=0, tiled=True)
    rest = [sum(pieces[1:], pieces[0]) for pieces in rest]
    columns, rest, received = lax.optimization_barrier((columns, rest, received))
    if rest:
        pieces, piece_tiles = next_tiles(rest[0], row_count, col_count)
    else:
        pieces = [columns[PANEL + t * TILE : PANEL + (t + 1) * TILE] for t in range(PANEL // TILE)]
        piece_tiles = [jnp.int32(t) for t in range(PANEL // TILE)]
    parts = [received] + [shift(received, "col", d, col_count) for d in range(1, col_count)]
    inverse = make_inverse(columns[:PANEL])
    panel, update = make_outputs(
        parts, pieces, piece_tiles, columns[:PANEL], inverse, share, row_count, col_count
    )
    shape_out = (image_rows * col_count // TILE, TILE, PANEL // TILE // col_count, TILE)
    return panel.reshape(shape_out), update.reshape(shape_out)


def solution(mesh):
    in_specs = (P(("row", "col"), None), P(), P(), P(), P(), P(("row", "col")))
    out_specs = (P(None, "row", None, "col"), P(None, "row", None, "col"))
    return jax.shard_map(
        per_device, mesh=mesh, in_specs=in_specs, out_specs=out_specs, check_vma=False
    )
```

```python
import functools

import jax
import jax.numpy as jnp
from jax import lax
from jax.experimental import pallas as pl
from jax.experimental.pallas import tpu as pltpu
from jax.sharding import PartitionSpec as P

TILE = 128
PANEL = 1024
META = 16
F32 = jnp.float32
BF16 = jnp.bfloat16
NN = (((1,), (0,)), ((), ()))
NT = (((1,), (1,)), ((), ()))
TN = (((0,), (0,)), ((), ()))

noise_var = 0.5


def iota(shape, dim):
    return lax.broadcasted_iota(jnp.int32, shape, dim)


def one_hot(cond):
    return jnp.where(cond, 1.0, 0.0).astype(BF16)


def dot(left, right, dims=NN):
    return lax.dot_general(left, right, dims, preferred_element_type=F32)


def split(value):
    high = value.astype(BF16)
    return high, (value - high.astype(F32)).astype(BF16)


def dot_split(left, right, dims=NN):
    return dot(left[0], right[0], dims) + (
        dot(left[0], right[1], dims) + dot(left[1], right[0], dims)
    )


def half_norms(feats):
    wide = feats.astype(F32)
    return 0.5 * jnp.sum(wide * wide, axis=1, keepdims=True)


def as_row(column):
    rows = column.shape[0]
    return jnp.broadcast_to(column, (rows, TILE)).T[:1, :]


def rbf(left, left_half, right, right_half_row):
    cross = dot(left, right, NT)
    return jnp.exp(jnp.minimum(cross - left_half - right_half_row, 0.0))


def feature_kernel(
    share, row_count, pos_ref, img_ref, win_ref, bias_ref, wout_ref, scale_ref, out_ref, acc_ref
):
    step = pl.program_id(0)
    preact = dot(img_ref[...], win_ref[...]) + bias_ref[...]
    hidden = 0.5 * preact * (1.0 + jnp.tanh(0.7978845608 * (preact + 0.044715 * preact * preact * preact)))
    part = dot(hidden.astype(BF16), wout_ref[...])

    @pl.when(step == 0)
    def _():
        acc_ref[...] = part

    @pl.when(step > 0)
    def _():
        acc_ref[...] += part

    @pl.when(step == pl.num_programs(0) - 1)
    def _():
        images = row_count * share
        feats = (acc_ref[...] * scale_ref[...]).astype(BF16)
        place = pos_ref[...]
        tile = place // TILE
        group = tile % row_count
        member = iota((row_count, images), 0) == group
        before = one_hot(iota((images, images), 0) < iota((images, images), 1))
        rank = dot(one_hot(member), before)
        target = jnp.where(member, rank + (share * iota((row_count, images), 0)).astype(F32), 0.0)
        target = jnp.sum(target, axis=0, keepdims=True).astype(jnp.int32)
        order = one_hot(iota((images, images), 0) == target)
        sorted_feats = dot(order, feats).astype(BF16)
        meta_row = iota((META, images), 0)
        meta = jnp.where(meta_row == 0, tile // row_count, jnp.where(meta_row == 1, place % TILE, 0))
        meta = meta.astype(F32).astype(BF16)
        lane = iota((TILE, images), 0) % share
        for r in range(row_count):
            out_ref[r, :share, :] = sorted_feats[r * share : (r + 1) * share, :]
            sel = one_hot(lane + r * share == target)
            spread = dot(meta, sel, NT).astype(BF16)
            out_ref[r, share:, :TILE] = spread
            out_ref[r, share:, TILE:] = jnp.zeros((META, out_ref.shape[2] - TILE), BF16)


def make_features(images, weight_in, bias_in, weight_out, feature_scale, position, row_count):
    rows, din = images.shape
    hid, feat = weight_out.shape
    share = rows // row_count
    block = 1024
    operands = (
        position.reshape(1, rows),
        images,
        weight_in,
        bias_in.reshape(1, hid),
        weight_out,
        feature_scale.reshape(1, feat),
    )
    return pl.pallas_call(
        functools.partial(feature_kernel, share, row_count),
        out_shape=jax.ShapeDtypeStruct((row_count, share + META, feat), BF16),
        grid=(hid // block,),
        in_specs=[
            pl.BlockSpec((1, rows), lambda i: (0, 0)),
            pl.BlockSpec((rows, din), lambda i: (0, 0)),
            pl.BlockSpec((din, block), lambda i: (0, i)),
            pl.BlockSpec((1, block), lambda i: (0, i)),
            pl.BlockSpec((block, feat), lambda i: (i, 0)),
            pl.BlockSpec((1, feat), lambda i: (0, 0)),
        ],
        out_specs=pl.BlockSpec((row_count, share + META, feat), lambda i: (0, 0, 0)),
        scratch_shapes=[pltpu.VMEM((rows, feat), F32)],
        compiler_params=pltpu.CompilerParams(vmem_limit_bytes=32 << 20),
        name="features",
    )(*[pltpu.with_memory_space_constraint(x, pltpu.HBM) for x in operands])


def read_slots(block_ref, lead, share, group):
    per = TILE // share
    lane = iota((META, TILE), 1) // share
    meta = None
    for j in range(per):
        piece = block_ref[lead + (group * per + j, slice(share, share + META), slice(0, TILE))].astype(F32)
        meta = piece if meta is None else jnp.where(lane == j, piece, meta)
    return (meta[0:1, :] * TILE + meta[1:2, :]).astype(jnp.int32)


def gather_rows(block_ref, lead, share, group):
    per = TILE // share
    return jnp.concatenate(
        [block_ref[lead + (group * per + j, slice(0, share), slice(None))] for j in range(per)], axis=0
    )


def lead_kernel(share, recv_ref, out_ref):
    groups = recv_ref.shape[0] * share // TILE
    slots = [read_slots(recv_ref, (), share, g) for g in range(groups)]
    rows = jnp.concatenate([gather_rows(recv_ref, (), share, g) for g in range(groups)], axis=0)
    shape = (out_ref.shape[0], TILE)
    pick = jnp.concatenate([one_hot(iota(shape, 0) == s) for s in slots], axis=1)
    out_ref[...] = dot(pick, rows).astype(BF16)


def make_lead(received, share, lead_tiles):
    return pl.pallas_call(
        functools.partial(lead_kernel, share),
        out_shape=jax.ShapeDtypeStruct((lead_tiles * TILE, received.shape[2]), BF16),
        name="lead",
    )(received)


def diag_inverse(block):
    size, width, ahead = block.shape[0], 8, 2
    count = size // width
    shape = (width, size)
    sub, lane = iota(shape, 0), iota(shape, 1)
    spread = lambda x: jnp.broadcast_to(x, shape)
    left = [block[q * width : (q + 1) * width, :] for q in range(count)]
    right = [jnp.where(lane == sub + q * width, 1.0, 0.0).astype(F32) for q in range(count)]
    columns = {}
    out = []
    for g in range(count):
        rows = range(g, min(g + ahead + 1, count))
        for q in rows:
            for h in range(g, min(q, g + ahead - 1) + 1):
                if (q, h) not in columns:
                    columns[q, h] = [spread(left[q][:, h * width + k : h * width + k + 1]) for k in range(width)]
        diag = jnp.ones(shape, F32)
        for i in range(width):
            own = spread(columns[g, g][i][i : i + 1, :])
            inv = 1.0 / own
            diag = jnp.where(sub == i, own, diag)
            source = {q: columns[q, g][i] for q in rows}
            factor = {q: source[q] * inv for q in rows}
            factor[g] = jnp.where(sub > i, factor[g], 0.0)
            for h in range(g, min(g + ahead, count)):
                for k in range(i + 1 if h == g else 0, width):
                    value = spread(source[h][k : k + 1, :])
                    for q in rows:
                        if q >= h:
                            columns[q, h][k] = columns[q, h][k] - factor[q] * value
            pivot_l, pivot_r = spread(left[g][i : i + 1, :]), spread(right[g][i : i + 1, :])
            for q in rows:
                left[q] = left[q] - factor[q] * pivot_l
                right[q] = right[q] - factor[q] * pivot_r
        scale = lax.rsqrt(diag)
        pivot_l, pivot_r = left[g] * scale, right[g] * scale
        out.append(pivot_r)
        first = g + ahead + 1
        if first < count:
            high = [x.astype(BF16).astype(F32) for x in (pivot_l, pivot_r)]
            low = [x - h for x, h in zip((pivot_l, pivot_r), high)]
            zero = jnp.zeros_like(pivot_l)
            lhs = jnp.concatenate([high[0], high[0], low[0], zero], axis=0).astype(BF16)
            high, low = jnp.concatenate(high, axis=1), jnp.concatenate(low, axis=1)
            rhs = jnp.concatenate([high, low, high, jnp.zeros_like(high)], axis=0).astype(BF16)
            gone = dot(lhs, rhs, TN)
            for q in range(first, count):
                left[q] = left[q] - gone[q * width : (q + 1) * width, :size]
                right[q] = right[q] - gone[q * width : (q + 1) * width, size:]
    return jnp.concatenate(out, axis=0)


def chol_kernel(cols_ref, out_ref, work_ref, high_ref, low_ref):
    blocks = PANEL // TILE
    feats = cols_ref[...]
    half = half_norms(feats)
    half_row = as_row(half)
    eye = iota((TILE, PANEL), 0) - iota((TILE, PANEL), 1)
    for k in range(blocks):
        rows = slice(k * TILE, (k + 1) * TILE)
        block = rbf(feats[rows], half[rows], feats, half_row)
        work_ref[rows, :] = block + jnp.where(eye == -k * TILE, noise_var, 0.0)
    lane = iota((TILE, PANEL), 1)

    def step(k, carry):
        base = pl.multiple_of(k * TILE, TILE)
        inverse = diag_inverse(work_ref[pl.ds(base, TILE), pl.ds(base, TILE)])
        work_ref[pl.ds(base, TILE), pl.ds(base, TILE)] = jnp.where(
            iota((TILE, TILE), 0) == iota((TILE, TILE), 1), 1.0, 0.0
        )
        row = dot_split(split(inverse), split(work_ref[pl.ds(base, TILE), :]))
        out_ref[pl.ds(base, TILE), :] = jnp.where(lane < base + TILE, row, 0.0)
        high, low = split(row)
        high_ref[...] = high
        low_ref[...] = low

        for done in range(1, blocks):

            @pl.when(k == done - 1)
            def _():
                rest = slice(done * TILE, PANEL)
                work_ref[rest, (done - 1) * TILE : done * TILE] = jnp.zeros((PANEL - done * TILE, TILE), F32)
                lower = (high_ref[:, rest], low_ref[:, rest])
                work_ref[rest, :] -= dot_split(lower, (high_ref[...], low_ref[...]), TN)

        return carry

    lax.fori_loop(0, blocks, step, 0)


def make_inverse(columns):
    return pl.pallas_call(
        chol_kernel,
        out_shape=jax.ShapeDtypeStruct((PANEL, PANEL), F32),
        scratch_shapes=[
            pltpu.VMEM((PANEL, PANEL), F32),
            pltpu.VMEM((TILE, PANEL), BF16),
            pltpu.VMEM((TILE, PANEL), BF16),
        ],
        compiler_params=pltpu.CompilerParams(vmem_limit_bytes=24 << 20),
        cost_estimate=pl.CostEstimate(flops=40 * 10**9, transcendentals=1 << 20, bytes_accessed=5 << 20),
        name="cholesky",
    )(columns)


def panel_kernel(share, row_count, col_count, rows_blk, parts, pieces, place_ref, *refs):
    recv_refs, next_refs = refs[:parts], refs[parts : parts + pieces]
    (cols_ref, inv_ref, panel_ref, update_ref, feats_ref, slots_ref, high_ref, half_ref,
     own_ref, own_half_ref) = refs[parts + pieces :]
    step = pl.program_id(0)
    row_index, col_index = place_ref[0], place_ref[1]
    col_tiles = PANEL // TILE // col_count
    width = col_tiles * TILE
    groups = recv_refs[0].shape[0] * share // TILE
    total = parts * groups

    @pl.when(step == 0)
    def _():
        for p in range(parts):
            for g in range(groups):
                q = p * groups + g
                slots_ref[:, q * TILE : (q + 1) * TILE] = jnp.broadcast_to(
                    read_slots(recv_refs[p], (), share, g), (8, TILE)
                )
                feats_ref[q * TILE : (q + 1) * TILE, :] = gather_rows(recv_refs[p], (), share, g)
        half_row = as_row(half_norms(cols_ref[...]))
        half_ref[...] = jnp.broadcast_to(half_row, (8, PANEL))
        inverse = split(inv_ref[...])
        own = []
        for t in range(col_tiles):
            tile = t * col_count + col_index
            for n, next_ref in enumerate(next_refs):

                @pl.when(place_ref[2 + n] == tile)
                def _():
                    own_ref[t * TILE : (t + 1) * TILE, :] = next_ref[...]

            own.append(inv_ref[pl.ds(pl.multiple_of(tile * TILE, TILE), TILE), :])
        own_feats = own_ref[...]
        own_half = half_norms(own_feats)
        own_half_ref[...] = jnp.broadcast_to(as_row(own_half), (8, width))
        cross = rbf(own_feats, own_half, cols_ref[...], half_row)
        solved = dot_split(split(dot_split(split(cross), inverse, NT)), inverse)
        right = jnp.concatenate(own + [solved], axis=0)
        high, low = split(right.T)
        high_ref[0:PANEL, :] = high
        high_ref[PANEL : 2 * PANEL, :] = low
        high_ref[2 * PANEL :, :] = high

    def body(diagonal):
        slot = iota((rows_blk, TILE), 0) + step * rows_blk
        pick = jnp.concatenate(
            [one_hot(slot == slots_ref[0:1, q * TILE : (q + 1) * TILE]) for q in range(total)], axis=1
        )
        feats = dot(pick, feats_ref[...]).astype(BF16)
        half = half_norms(feats)
        kern = rbf(feats, half, cols_ref[...], half_ref[0:1, :])
        kern_next = rbf(feats, half, own_ref[...], own_half_ref[0:1, :])
        if diagonal:
            local = iota((rows_blk, 1), 0) + step * rows_blk
            place = (local // TILE * row_count + row_index) * TILE + local % TILE
            kern = kern + jnp.where(place == iota((rows_blk, PANEL), 1), noise_var, 0.0)
            index = iota((rows_blk, width), 1)
            column = PANEL + (index // TILE * col_count + col_index) * TILE + index % TILE
            kern_next = kern_next + jnp.where(place == column, noise_var, 0.0)
        high, low = split(kern)
        result = dot(jnp.concatenate([high, high, low], axis=1), high_ref[...])
        update = kern_next - result[:, width:]
        for t in range(col_tiles):
            where = pl.ds(t, rows_blk, stride=col_tiles) if col_tiles > 1 else slice(None)
            panel_ref[where, :] = result[:, t * TILE : (t + 1) * TILE]
            update_ref[where, :] = update[:, t * TILE : (t + 1) * TILE]

    lead_rows = max(2 * PANEL // row_count, TILE)
    has_diag = step * rows_blk < lead_rows

    @pl.when(has_diag)
    def _():
        body(True)

    @pl.when(jnp.logical_not(has_diag))
    def _():
        body(False)


def make_outputs(parts, pieces, piece_tiles, columns, inverse, share, row_count, col_count):
    feat = columns.shape[1]
    local_rows = len(parts) * parts[0].shape[0] * share
    col_tiles = PANEL // TILE // col_count
    width = col_tiles * TILE
    rows_blk = 512
    place = jnp.stack([lax.axis_index("row"), lax.axis_index("col")] + piece_tiles).astype(jnp.int32)
    operands = (*parts, *pieces, columns, inverse)
    out = jax.ShapeDtypeStruct((local_rows * col_tiles, TILE), F32)
    out_spec = pl.BlockSpec((rows_blk * col_tiles, TILE), lambda i, s: (i, 0))
    return pl.pallas_call(
        functools.partial(panel_kernel, share, row_count, col_count, rows_blk, len(parts), len(pieces)),
        out_shape=[out, out],
        grid_spec=pltpu.PrefetchScalarGridSpec(
            num_scalar_prefetch=1,
            grid=(local_rows // rows_blk,),
            in_specs=[pl.BlockSpec(memory_space=pltpu.VMEM)] * len(operands),
            out_specs=[out_spec, out_spec],
            scratch_shapes=[
                pltpu.VMEM((local_rows, feat), BF16),
                pltpu.VMEM((8, local_rows), jnp.int32),
                pltpu.VMEM((3 * PANEL, 2 * width), BF16),
                pltpu.VMEM((8, PANEL), F32),
                pltpu.VMEM((width, feat), BF16),
                pltpu.VMEM((8, width), F32),
            ],
        ),
        compiler_params=pltpu.CompilerParams(vmem_limit_bytes=36 << 20),
        name="panels",
    )(place, *operands)


def shift(value, axis, distance, size):
    return lax.ppermute(value, axis, [(i, (i + distance) % size) for i in range(size)])


def exchange(value, axis, step, size):
    return lax.ppermute(value, axis, [(i, i ^ step) for i in range(size)])


def sum_over(value, axis, size):
    step = 1
    while step < size:
        value = value + exchange(value, axis, step, size)
        step *= 2
    return value


def next_tiles(tile, row_count, col_count):
    turns = PANEL // TILE // col_count
    row_index, col_index = lax.axis_index("row"), lax.axis_index("col")
    pieces, piece_tiles = [], []
    for turn in range(turns):
        pairs = []
        for r in range(row_count):
            for c in range(col_count):
                owner = c + col_count * ((r // col_count + turn) % turns)
                pairs.append((owner * col_count + r % col_count, r * col_count + c))
        pieces.append(lax.ppermute(tile, ("row", "col"), pairs))
        piece_tiles.append(col_index + col_count * ((row_index // col_count + turn) % turns))
    return pieces, piece_tiles


def per_device(images, weight_in, bias_in, weight_out, feature_scale, position):
    image_rows = images.shape[0]
    feat = weight_out.shape[1]
    row_count = lax.axis_size("row")
    col_count = lax.axis_size("col")
    share = image_rows // row_count
    lead_tiles = 2 * PANEL // (TILE * row_count)
    bucket = make_features(
        images, weight_in, bias_in, weight_out, feature_scale, position, row_count
    )
    received = lax.all_to_all(bucket, "row", split_axis=0, concat_axis=0, tiled=True)
    lead = make_lead(received, share, lead_tiles)
    lead = sum_over(lead, "col", col_count)
    lead, received = lax.optimization_barrier((lead, received))
    parts = [received] + [shift(received, "col", d, col_count) for d in range(1, col_count)]
    if lead_tiles > 1:
        pieces, piece_tiles = next_tiles(lead[TILE : 2 * TILE], row_count, col_count)
    columns = lax.all_gather(lead[:TILE], "row", axis=0, tiled=True)
    if lead_tiles == 1:
        pieces = [columns[PANEL + t * TILE : PANEL + (t + 1) * TILE] for t in range(PANEL // TILE)]
        piece_tiles = [jnp.int32(t) for t in range(PANEL // TILE)]
    inverse = make_inverse(columns[:PANEL])
    panel, update = make_outputs(
        parts, pieces, piece_tiles, columns[:PANEL], inverse, share, row_count, col_count
    )
    shape_out = (image_rows * col_count // TILE, TILE, PANEL // TILE // col_count, TILE)
    return panel.reshape(shape_out), update.reshape(shape_out)


def solution(mesh):
    in_specs = (P(("row", "col"), None), P(), P(), P(), P(), P(("row", "col")))
    out_specs = (P(None, "row", None, "col"), P(None, "row", None, "col"))
    return jax.shard_map(
        per_device, mesh=mesh, in_specs=in_specs, out_specs=out_specs, check_vma=False
    )
```

```python
import functools

import jax
import jax.numpy as jnp
from jax import lax
from jax.experimental import pallas as pl
from jax.experimental.pallas import tpu as pltpu
from jax.sharding import PartitionSpec as P

TILE = 128
PANEL = 1024
META = 16
F32 = jnp.float32
BF16 = jnp.bfloat16
NN = (((1,), (0,)), ((), ()))
NT = (((1,), (1,)), ((), ()))
TN = (((0,), (0,)), ((), ()))

noise_var = 0.5


def iota(shape, dim):
    return lax.broadcasted_iota(jnp.int32, shape, dim)


def one_hot(cond):
    return jnp.where(cond, 1.0, 0.0).astype(BF16)


def dot(left, right, dims=NN):
    return lax.dot_general(left, right, dims, preferred_element_type=F32)


def split(value):
    high = value.astype(BF16)
    return high, (value - high.astype(F32)).astype(BF16)


def dot_split(left, right, dims=NN):
    return dot(left[0], right[0], dims) + (
        dot(left[0], right[1], dims) + dot(left[1], right[0], dims)
    )


def half_norms(feats):
    wide = feats.astype(F32)
    return 0.5 * jnp.sum(wide * wide, axis=1, keepdims=True)


def as_row(column):
    rows = column.shape[0]
    return jnp.broadcast_to(column, (rows, TILE)).T[:1, :]


def rbf(left, left_half, right, right_half_row):
    cross = dot(left, right, NT)
    return jnp.exp(jnp.minimum(cross - left_half - right_half_row, 0.0))


def feature_kernel(
    share, row_count, pos_ref, img_ref, win_ref, bias_ref, wout_ref, scale_ref, out_ref, acc_ref
):
    step = pl.program_id(0)
    preact = dot(img_ref[...], win_ref[...]) + bias_ref[...]
    hidden = 0.5 * preact * (1.0 + jnp.tanh(0.7978845608 * (preact + 0.044715 * preact * preact * preact)))
    part = dot(hidden.astype(BF16), wout_ref[...])

    @pl.when(step == 0)
    def _():
        acc_ref[...] = part

    @pl.when(step > 0)
    def _():
        acc_ref[...] += part

    @pl.when(step == pl.num_programs(0) - 1)
    def _():
        images = row_count * share
        feats = (acc_ref[...] * scale_ref[...]).astype(BF16)
        place = pos_ref[...]
        tile = place // TILE
        group = tile % row_count
        member = iota((row_count, images), 0) == group
        before = one_hot(iota((images, images), 0) < iota((images, images), 1))
        rank = dot(one_hot(member), before)
        target = jnp.where(member, rank + (share * iota((row_count, images), 0)).astype(F32), 0.0)
        target = jnp.sum(target, axis=0, keepdims=True).astype(jnp.int32)
        order = one_hot(iota((images, images), 0) == target)
        sorted_feats = dot(order, feats).astype(BF16)
        meta_row = iota((META, images), 0)
        meta = jnp.where(meta_row == 0, tile // row_count, jnp.where(meta_row == 1, place % TILE, 0))
        meta = meta.astype(F32).astype(BF16)
        lane = iota((TILE, images), 0) % share
        for r in range(row_count):
            out_ref[r, :share, :] = sorted_feats[r * share : (r + 1) * share, :]
            sel = one_hot(lane + r * share == target)
            spread = dot(meta, sel, NT).astype(BF16)
            out_ref[r, share:, :TILE] = spread
            out_ref[r, share:, TILE:] = jnp.zeros((META, out_ref.shape[2] - TILE), BF16)


def make_features(images, weight_in, bias_in, weight_out, feature_scale, position, row_count):
    rows, din = images.shape
    hid, feat = weight_out.shape
    share = rows // row_count
    block = 1024
    operands = (
        position.reshape(1, rows),
        images,
        weight_in,
        bias_in.reshape(1, hid),
        weight_out,
        feature_scale.reshape(1, feat),
    )
    return pl.pallas_call(
        functools.partial(feature_kernel, share, row_count),
        out_shape=jax.ShapeDtypeStruct((row_count, share + META, feat), BF16),
        grid=(hid // block,),
        in_specs=[
            pl.BlockSpec((1, rows), lambda i: (0, 0)),
            pl.BlockSpec((rows, din), lambda i: (0, 0)),
            pl.BlockSpec((din, block), lambda i: (0, i)),
            pl.BlockSpec((1, block), lambda i: (0, i)),
            pl.BlockSpec((block, feat), lambda i: (i, 0)),
            pl.BlockSpec((1, feat), lambda i: (0, 0)),
        ],
        out_specs=pl.BlockSpec((row_count, share + META, feat), lambda i: (0, 0, 0)),
        scratch_shapes=[pltpu.VMEM((rows, feat), F32)],
        compiler_params=pltpu.CompilerParams(vmem_limit_bytes=32 << 20),
        name="features",
    )(*[pltpu.with_memory_space_constraint(x, pltpu.HBM) for x in operands])


def read_slots(block_ref, lead, share, group):
    per = TILE // share
    lane = iota((META, TILE), 1) // share
    meta = None
    for j in range(per):
        piece = block_ref[lead + (group * per + j, slice(share, share + META), slice(0, TILE))].astype(F32)
        meta = piece if meta is None else jnp.where(lane == j, piece, meta)
    return (meta[0:1, :] * TILE + meta[1:2, :]).astype(jnp.int32)


def gather_rows(block_ref, lead, share, group):
    per = TILE // share
    return jnp.concatenate(
        [block_ref[lead + (group * per + j, slice(0, share), slice(None))] for j in range(per)], axis=0
    )


def lead_kernel(share, recv_ref, out_ref):
    groups = recv_ref.shape[0] * share // TILE
    slots = [read_slots(recv_ref, (), share, g) for g in range(groups)]
    rows = jnp.concatenate([gather_rows(recv_ref, (), share, g) for g in range(groups)], axis=0)
    shape = (out_ref.shape[0], TILE)
    pick = jnp.concatenate([one_hot(iota(shape, 0) == s) for s in slots], axis=1)
    out_ref[...] = dot(pick, rows).astype(BF16)


def make_lead(received, share, lead_tiles):
    return pl.pallas_call(
        functools.partial(lead_kernel, share),
        out_shape=jax.ShapeDtypeStruct((lead_tiles * TILE, received.shape[2]), BF16),
        name="lead",
    )(received)


def diag_inverse(block):
    size, width, ahead = block.shape[0], 8, 3
    count = size // width
    shape = (width, size)
    sub, lane = iota(shape, 0), iota(shape, 1)
    spread = lambda x: jnp.broadcast_to(x, shape)
    work = [block[q * width : (q + 1) * width, :] for q in range(count)]
    columns = {}
    out = []
    for g in range(count):
        base, first = g * width, g + ahead + 1
        rows = range(g, min(first, count))
        for q in rows:
            for h in range(g, min(q, g + 1) + 1):
                if (q, h) not in columns:
                    columns[q, h] = [spread(work[q][:, h * width + k : h * width + k + 1]) for k in range(width)]
        pivot_lane = (lane >= base) & (lane < base + width)
        for q in rows:
            start = jnp.where(lane - base == sub, 1.0, 0.0) if q == g else 0.0
            work[q] = jnp.where(pivot_lane, start, work[q])
        diag = jnp.ones(shape, F32)
        for i in range(width):
            own = spread(columns[g, g][i][i : i + 1, :])
            inv = 1.0 / own
            diag = jnp.where(sub == i, own, diag)
            source = {q: columns[q, g][i] for q in rows}
            factor = {q: source[q] * inv for q in rows}
            factor[g] = jnp.where(sub > i, factor[g], 0.0)
            for h in range(g, min(g + 2, count)):
                for k in range(i + 1 if h == g else 0, width):
                    value = spread(source[h][k : k + 1, :])
                    for q in rows:
                        if q >= h:
                            columns[q, h][k] = columns[q, h][k] - factor[q] * value
            pivot = spread(work[g][i : i + 1, :])
            for q in rows:
                work[q] = work[q] - factor[q] * pivot
        scaled = work[g] * lax.rsqrt(diag)
        out.append(jnp.where(lane < base + width, scaled, 0.0))
        if first < count:
            high = scaled.astype(BF16).astype(F32)
            low = scaled - high
            zero = jnp.zeros_like(high)
            lhs = jnp.concatenate([high, high, low, zero], axis=0).astype(BF16)
            rhs = jnp.concatenate([high, low, high, zero], axis=0).astype(BF16)
            gone = dot(lhs, rhs, TN)
            for q in range(first, count):
                work[q] = jnp.where(pivot_lane, 0.0, work[q]) - gone[q * width : (q + 1) * width, :]
    return jnp.concatenate(out, axis=0)


def chol_kernel(cols_ref, out_ref, work_ref, high_ref, low_ref):
    blocks = PANEL // TILE
    feats = cols_ref[...]
    half = half_norms(feats)
    half_row = as_row(half)
    chunk = 2 * TILE
    for top in range(0, PANEL, chunk):
        rows, cols = slice(top, top + chunk), slice(top, PANEL)
        block = rbf(feats[rows], half[rows], feats[cols], half_row[:, cols])
        eye = iota(block.shape, 0) == iota(block.shape, 1)
        work_ref[rows, cols] = block + jnp.where(eye, noise_var, 0.0)
        if top:
            work_ref[rows, :top] = jnp.zeros((chunk, top), F32)
    lane = iota((TILE, PANEL), 1)

    def step(k, carry):
        base = pl.multiple_of(k * TILE, TILE)
        inverse = diag_inverse(work_ref[pl.ds(base, TILE), pl.ds(base, TILE)])
        work_ref[pl.ds(base, TILE), pl.ds(base, TILE)] = jnp.where(
            iota((TILE, TILE), 0) == iota((TILE, TILE), 1), 1.0, 0.0
        )
        row = dot_split(split(inverse), split(work_ref[pl.ds(base, TILE), :]))
        out_ref[pl.ds(base, TILE), :] = jnp.where(lane < base + TILE, row, 0.0)
        high, low = split(row)
        high_ref[:TILE, :] = high
        high_ref[TILE : 2 * TILE, :] = low
        high_ref[2 * TILE :, :] = high
        low_ref[:TILE, :] = high
        low_ref[TILE : 2 * TILE, :] = high
        low_ref[2 * TILE :, :] = low

        for done in range(1, blocks):

            @pl.when(k == done - 1)
            def _():
                rest = slice(done * TILE, PANEL)
                work_ref[rest, (done - 1) * TILE : done * TILE] = jnp.zeros((PANEL - done * TILE, TILE), F32)
                for top in range(done * TILE, PANEL, 2 * TILE):
                    part = slice(top, min(top + 2 * TILE, PANEL))
                    near, far = slice(0, done * TILE), slice(top, PANEL)
                    work_ref[part, near] -= dot(low_ref[:, part], high_ref[:, near], TN)
                    work_ref[part, far] -= dot(low_ref[:, part], high_ref[:, far], TN)

        return carry

    lax.fori_loop(0, blocks, step, 0)


def make_inverse(columns):
    return pl.pallas_call(
        chol_kernel,
        out_shape=jax.ShapeDtypeStruct((PANEL, PANEL), F32),
        scratch_shapes=[
            pltpu.VMEM((PANEL, PANEL), F32),
            pltpu.VMEM((3 * TILE, PANEL), BF16),
            pltpu.VMEM((3 * TILE, PANEL), BF16),
        ],
        compiler_params=pltpu.CompilerParams(vmem_limit_bytes=24 << 20),
        cost_estimate=pl.CostEstimate(flops=40 * 10**9, transcendentals=1 << 20, bytes_accessed=5 << 20),
        name="cholesky",
    )(columns)


def panel_kernel(share, row_count, col_count, rows_blk, parts, pieces, place_ref, *refs):
    recv_refs, next_refs = refs[:parts], refs[parts : parts + pieces]
    (cols_ref, inv_ref, panel_ref, update_ref, feats_ref, slots_ref, high_ref, half_ref,
     own_ref, own_half_ref) = refs[parts + pieces :]
    step = pl.program_id(0)
    row_index, col_index = place_ref[0], place_ref[1]
    col_tiles = PANEL // TILE // col_count
    width = col_tiles * TILE
    groups = recv_refs[0].shape[0] * share // TILE
    total = parts * groups

    @pl.when(step == 0)
    def _():
        for p in range(parts):
            for g in range(groups):
                q = p * groups + g
                slots_ref[:, q * TILE : (q + 1) * TILE] = jnp.broadcast_to(
                    read_slots(recv_refs[p], (), share, g), (8, TILE)
                )
                feats_ref[q * TILE : (q + 1) * TILE, :] = gather_rows(recv_refs[p], (), share, g)
        half_row = as_row(half_norms(cols_ref[...]))
        half_ref[...] = jnp.broadcast_to(half_row, (8, PANEL))
        inverse = split(inv_ref[...])
        own = []
        for t in range(col_tiles):
            tile = t * col_count + col_index
            for n, next_ref in enumerate(next_refs):

                @pl.when(place_ref[2 + n] == tile)
                def _():
                    own_ref[t * TILE : (t + 1) * TILE, :] = next_ref[...]

            own.append(inv_ref[pl.ds(pl.multiple_of(tile * TILE, TILE), TILE), :])
        own_feats = own_ref[...]
        own_half = half_norms(own_feats)
        own_half_ref[...] = jnp.broadcast_to(as_row(own_half), (8, width))
        cross = rbf(own_feats, own_half, cols_ref[...], half_row)
        solved = dot_split(split(dot_split(split(cross), inverse, NT)), inverse)
        right = jnp.concatenate(own + [solved], axis=0)
        high, low = split(right.T)
        high_ref[0:PANEL, :] = high
        high_ref[PANEL : 2 * PANEL, :] = low
        high_ref[2 * PANEL :, :] = high

    def body(diagonal):
        slot = iota((rows_blk, TILE), 0) + step * rows_blk
        pick = jnp.concatenate(
            [one_hot(slot == slots_ref[0:1, q * TILE : (q + 1) * TILE]) for q in range(total)], axis=1
        )
        feats = dot(pick, feats_ref[...]).astype(BF16)
        half = half_norms(feats)
        kern = rbf(feats, half, cols_ref[...], half_ref[0:1, :])
        kern_next = rbf(feats, half, own_ref[...], own_half_ref[0:1, :])
        if diagonal:
            local = iota((rows_blk, 1), 0) + step * rows_blk
            place = (local // TILE * row_count + row_index) * TILE + local % TILE
            kern = kern + jnp.where(place == iota((rows_blk, PANEL), 1), noise_var, 0.0)
            index = iota((rows_blk, width), 1)
            column = PANEL + (index // TILE * col_count + col_index) * TILE + index % TILE
            kern_next = kern_next + jnp.where(place == column, noise_var, 0.0)
        high, low = split(kern)
        result = dot(jnp.concatenate([high, high, low], axis=1), high_ref[...])
        update = kern_next - result[:, width:]
        for t in range(col_tiles):
            where = pl.ds(t, rows_blk, stride=col_tiles) if col_tiles > 1 else slice(None)
            panel_ref[where, :] = result[:, t * TILE : (t + 1) * TILE]
            update_ref[where, :] = update[:, t * TILE : (t + 1) * TILE]

    lead_rows = max(2 * PANEL // row_count, TILE)
    has_diag = step * rows_blk < lead_rows

    @pl.when(has_diag)
    def _():
        body(True)

    @pl.when(jnp.logical_not(has_diag))
    def _():
        body(False)


def make_outputs(parts, pieces, piece_tiles, columns, inverse, share, row_count, col_count):
    feat = columns.shape[1]
    local_rows = len(parts) * parts[0].shape[0] * share
    col_tiles = PANEL // TILE // col_count
    width = col_tiles * TILE
    rows_blk = 512
    place = jnp.stack([lax.axis_index("row"), lax.axis_index("col")] + piece_tiles).astype(jnp.int32)
    operands = (*parts, *pieces, columns, inverse)
    out = jax.ShapeDtypeStruct((local_rows * col_tiles, TILE), F32)
    out_spec = pl.BlockSpec((rows_blk * col_tiles, TILE), lambda i, s: (i, 0))
    return pl.pallas_call(
        functools.partial(panel_kernel, share, row_count, col_count, rows_blk, len(parts), len(pieces)),
        out_shape=[out, out],
        grid_spec=pltpu.PrefetchScalarGridSpec(
            num_scalar_prefetch=1,
            grid=(local_rows // rows_blk,),
            in_specs=[pl.BlockSpec(memory_space=pltpu.VMEM)] * len(operands),
            out_specs=[out_spec, out_spec],
            scratch_shapes=[
                pltpu.VMEM((local_rows, feat), BF16),
                pltpu.VMEM((8, local_rows), jnp.int32),
                pltpu.VMEM((3 * PANEL, 2 * width), BF16),
                pltpu.VMEM((8, PANEL), F32),
                pltpu.VMEM((width, feat), BF16),
                pltpu.VMEM((8, width), F32),
            ],
        ),
        compiler_params=pltpu.CompilerParams(vmem_limit_bytes=36 << 20),
        name="panels",
    )(place, *operands)


def shift(value, axis, distance, size):
    return lax.ppermute(value, axis, [(i, (i + distance) % size) for i in range(size)])


def exchange(value, axis, step, size):
    return lax.ppermute(value, axis, [(i, i ^ step) for i in range(size)])


def sum_over(value, axis, size):
    step = 1
    while step < size:
        value = value + exchange(value, axis, step, size)
        step *= 2
    return value


def next_tiles(tile, row_count, col_count):
    turns = PANEL // TILE // col_count
    row_index, col_index = lax.axis_index("row"), lax.axis_index("col")
    pieces, piece_tiles = [], []
    for turn in range(turns):
        pairs = []
        for r in range(row_count):
            for c in range(col_count):
                owner = c + col_count * ((r // col_count + turn) % turns)
                pairs.append((owner * col_count + r % col_count, r * col_count + c))
        pieces.append(lax.ppermute(tile, ("row", "col"), pairs))
        piece_tiles.append(col_index + col_count * ((row_index // col_count + turn) % turns))
    return pieces, piece_tiles


def per_device(images, weight_in, bias_in, weight_out, feature_scale, position):
    image_rows = images.shape[0]
    feat = weight_out.shape[1]
    row_count = lax.axis_size("row")
    col_count = lax.axis_size("col")
    share = image_rows // row_count
    lead_tiles = 2 * PANEL // (TILE * row_count)
    bucket = make_features(
        images, weight_in, bias_in, weight_out, feature_scale, position, row_count
    )
    received = lax.all_to_all(bucket, "row", split_axis=0, concat_axis=0, tiled=True)
    lead = make_lead(received, share, lead_tiles)
    lead = sum_over(lead, "col", col_count)
    lead, received = lax.optimization_barrier((lead, received))
    parts = [received] + [shift(received, "col", d, col_count) for d in range(1, col_count)]
    columns = lax.all_gather(lead[:TILE], "row", axis=0, tiled=True)
    if lead_tiles > 1:
        lead, columns = lax.optimization_barrier((lead, columns))
        pieces, piece_tiles = next_tiles(lead[TILE : 2 * TILE], row_count, col_count)
    else:
        pieces = [columns[PANEL + t * TILE : PANEL + (t + 1) * TILE] for t in range(PANEL // TILE)]
        piece_tiles = [jnp.int32(t) for t in range(PANEL // TILE)]
    inverse = make_inverse(columns[:PANEL])
    panel, update = make_outputs(
        parts, pieces, piece_tiles, columns[:PANEL], inverse, share, row_count, col_count
    )
    shape_out = (image_rows * col_count // TILE, TILE, PANEL // TILE // col_count, TILE)
    return panel.reshape(shape_out), update.reshape(shape_out)


def solution(mesh):
    in_specs = (P(("row", "col"), None), P(), P(), P(), P(), P(("row", "col")))
    out_specs = (P(None, "row", None, "col"), P(None, "row", None, "col"))
    return jax.shard_map(
        per_device, mesh=mesh, in_specs=in_specs, out_specs=out_specs, check_vma=False
    )
```

```python
import functools

import jax
import jax.numpy as jnp
from jax import lax
from jax.experimental import pallas as pl
from jax.experimental.pallas import tpu as pltpu
from jax.sharding import PartitionSpec as P

TILE = 128
PANEL = 1024
META = 8
F32 = jnp.float32
BF16 = jnp.bfloat16
NN = (((1,), (0,)), ((), ()))
NT = (((1,), (1,)), ((), ()))
TN = (((0,), (0,)), ((), ()))

noise_var = 0.5


def iota(shape, dim):
    return lax.broadcasted_iota(jnp.int32, shape, dim)


def one_hot(cond):
    return jnp.where(cond, 1.0, 0.0).astype(BF16)


def dot(left, right, dims=NN):
    return lax.dot_general(left, right, dims, preferred_element_type=F32)


def split(value):
    high = value.astype(BF16)
    return high, (value - high.astype(F32)).astype(BF16)


def dot_split(left, right, dims=NN):
    return dot(left[0], right[0], dims) + (
        dot(left[0], right[1], dims) + dot(left[1], right[0], dims)
    )


def half_norms(feats):
    wide = feats.astype(F32)
    return 0.5 * jnp.sum(wide * wide, axis=1, keepdims=True)


def as_row(column):
    rows = column.shape[0]
    return jnp.broadcast_to(column, (rows, TILE)).T[:1, :]


def rbf(left, left_half, right, right_half_row):
    cross = dot(left, right, NT)
    return jnp.exp(jnp.minimum(cross - left_half - right_half_row, 0.0))


def feature_kernel(
    share, row_count, pos_ref, img_ref, win_ref, bias_ref, wout_ref, scale_ref, out_ref, acc_ref
):
    step = pl.program_id(0)
    preact = dot(img_ref[...], win_ref[...]) + bias_ref[...]
    inner = preact * (0.7978845608 + 0.7978845608 * 0.044715 * preact * preact)
    half = 0.5 * preact
    hidden = half + half * jnp.tanh(inner)
    part = dot(hidden.astype(BF16), wout_ref[...])

    @pl.when(step == 0)
    def _():
        acc_ref[...] = part

    @pl.when(step > 0)
    def _():
        acc_ref[...] += part

    @pl.when(step == pl.num_programs(0) - 1)
    def _():
        images = row_count * share
        feats = (acc_ref[...] * scale_ref[...]).astype(BF16)
        place = pos_ref[...]
        tile = place // TILE
        group = tile % row_count
        member = iota((row_count, images), 0) == group
        before = one_hot(iota((images, images), 0) < iota((images, images), 1))
        rank = dot(one_hot(member), before)
        target = jnp.where(member, rank + (share * iota((row_count, images), 0)).astype(F32), 0.0)
        target = jnp.sum(target, axis=0, keepdims=True).astype(jnp.int32)
        order = one_hot(iota((images, images), 0) == target)
        sorted_feats = dot(order, feats).astype(BF16)
        meta_row = iota((META, images), 0)
        meta = jnp.where(meta_row == 0, tile // row_count, jnp.where(meta_row == 1, place % TILE, 0))
        meta = meta.astype(F32).astype(BF16)
        lane = iota((TILE, images), 0) % share
        for r in range(row_count):
            out_ref[r, :share, :] = sorted_feats[r * share : (r + 1) * share, :]
            sel = one_hot(lane + r * share == target)
            spread = dot(meta, sel, NT).astype(BF16)
            out_ref[r, share:, :TILE] = spread
            out_ref[r, share:, TILE:] = jnp.zeros((META, out_ref.shape[2] - TILE), BF16)


def make_features(images, weight_in, bias_in, weight_out, feature_scale, position, row_count):
    rows, din = images.shape
    hid, feat = weight_out.shape
    share = rows // row_count
    block = 1024
    operands = (
        position.reshape(1, rows),
        images,
        weight_in,
        bias_in.reshape(1, hid),
        weight_out,
        feature_scale.reshape(1, feat),
    )
    return pl.pallas_call(
        functools.partial(feature_kernel, share, row_count),
        out_shape=jax.ShapeDtypeStruct((row_count, share + META, feat), BF16),
        grid=(hid // block,),
        in_specs=[
            pl.BlockSpec((1, rows), lambda i: (0, 0)),
            pl.BlockSpec((rows, din), lambda i: (0, 0)),
            pl.BlockSpec((din, block), lambda i: (0, i)),
            pl.BlockSpec((1, block), lambda i: (0, i)),
            pl.BlockSpec((block, feat), lambda i: (i, 0)),
            pl.BlockSpec((1, feat), lambda i: (0, 0)),
        ],
        out_specs=pl.BlockSpec((row_count, share + META, feat), lambda i: (0, 0, 0)),
        scratch_shapes=[pltpu.VMEM((rows, feat), F32)],
        compiler_params=pltpu.CompilerParams(vmem_limit_bytes=32 << 20),
        name="features",
    )(*[pltpu.with_memory_space_constraint(x, pltpu.HBM) for x in operands])


def read_slots(block_ref, lead, share, group):
    per = TILE // share
    lane = iota((META, TILE), 1) // share
    meta = None
    for j in range(per):
        piece = block_ref[lead + (group * per + j, slice(share, share + META), slice(0, TILE))].astype(F32)
        meta = piece if meta is None else jnp.where(lane == j, piece, meta)
    return (meta[0:1, :] * TILE + meta[1:2, :]).astype(jnp.int32)


def gather_rows(block_ref, lead, share, group):
    per = TILE // share
    return jnp.concatenate(
        [block_ref[lead + (group * per + j, slice(0, share), slice(None))] for j in range(per)], axis=0
    )


def lead_kernel(share, recv_ref, out_ref):
    groups = recv_ref.shape[0] * share // TILE
    slots = [read_slots(recv_ref, (), share, g) for g in range(groups)]
    rows = jnp.concatenate([gather_rows(recv_ref, (), share, g) for g in range(groups)], axis=0)
    shape = (out_ref.shape[0], TILE)
    pick = jnp.concatenate([one_hot(iota(shape, 0) == s) for s in slots], axis=1)
    out_ref[...] = dot(pick, rows).astype(BF16)


def make_lead(received, share, lead_tiles):
    return pl.pallas_call(
        functools.partial(lead_kernel, share),
        out_shape=jax.ShapeDtypeStruct((lead_tiles * TILE, received.shape[2]), BF16),
        name="lead",
    )(received)


def diag_inverse(block):
    size, width, ahead = block.shape[0], 8, 3
    count = size // width
    shape = (width, size)
    sub, lane = iota(shape, 0), iota(shape, 1)
    spread = lambda x: jnp.broadcast_to(x, shape)
    work = [block[q * width : (q + 1) * width, :] for q in range(count)]
    columns = {}
    out = []
    for g in range(count):
        base, first = g * width, g + ahead + 1
        rows = range(g, min(first, count))
        for q in rows:
            for h in range(g, min(q, g + 1) + 1):
                if (q, h) not in columns:
                    columns[q, h] = [spread(work[q][:, h * width + k : h * width + k + 1]) for k in range(width)]
        pivot_lane = (lane >= base) & (lane < base + width)
        for q in rows:
            start = jnp.where(lane - base == sub, 1.0, 0.0) if q == g else 0.0
            work[q] = jnp.where(pivot_lane, start, work[q])
        diag = jnp.ones(shape, F32)
        for i in range(width):
            own = spread(columns[g, g][i][i : i + 1, :])
            inv = 1.0 / own
            diag = jnp.where(sub == i, own, diag)
            source = {q: columns[q, g][i] for q in rows}
            factor = {q: source[q] * inv for q in rows}
            factor[g] = jnp.where(sub > i, factor[g], 0.0)
            for h in range(g, min(g + 2, count)):
                for k in range(i + 1 if h == g else 0, width):
                    value = spread(source[h][k : k + 1, :])
                    for q in rows:
                        if q >= h:
                            columns[q, h][k] = columns[q, h][k] - factor[q] * value
            pivot = spread(work[g][i : i + 1, :])
            for q in rows:
                work[q] = work[q] - factor[q] * pivot
        scaled = work[g] * lax.rsqrt(diag)
        out.append(jnp.where(lane < base + width, scaled, 0.0))
        if first < count:
            high = scaled.astype(BF16).astype(F32)
            low = scaled - high
            zero = jnp.zeros_like(high)
            lhs = jnp.concatenate([high, high, low, zero], axis=0).astype(BF16)
            rhs = jnp.concatenate([high, low, high, zero], axis=0).astype(BF16)
            gone = dot(lhs, rhs, TN)
            for q in range(first, count):
                work[q] = jnp.where(pivot_lane, 0.0, work[q]) - gone[q * width : (q + 1) * width, :]
    return jnp.concatenate(out, axis=0)


def chol_kernel(cols_ref, out_ref, work_ref, high_ref, low_ref):
    blocks = PANEL // TILE
    feats = cols_ref[...]
    half = half_norms(feats)
    half_row = as_row(half)
    chunk = 2 * TILE
    for top in range(0, PANEL, chunk):
        rows, cols = slice(top, top + chunk), slice(top, PANEL)
        block = rbf(feats[rows], half[rows], feats[cols], half_row[:, cols])
        eye = iota(block.shape, 0) == iota(block.shape, 1)
        work_ref[rows, cols] = block + jnp.where(eye, noise_var, 0.0)
        if top:
            work_ref[rows, :top] = jnp.zeros((chunk, top), F32)
    lane = iota((TILE, PANEL), 1)

    def step(k, carry):
        base = pl.multiple_of(k * TILE, TILE)
        inverse = diag_inverse(work_ref[pl.ds(base, TILE), pl.ds(base, TILE)])
        work_ref[pl.ds(base, TILE), pl.ds(base, TILE)] = jnp.where(
            iota((TILE, TILE), 0) == iota((TILE, TILE), 1), 1.0, 0.0
        )
        row = dot_split(split(inverse), split(work_ref[pl.ds(base, TILE), :]))
        out_ref[pl.ds(base, TILE), :] = jnp.where(lane < base + TILE, row, 0.0)
        high, low = split(row)
        high_ref[:TILE, :] = high
        high_ref[TILE : 2 * TILE, :] = low
        high_ref[2 * TILE :, :] = high
        low_ref[:TILE, :] = high
        low_ref[TILE : 2 * TILE, :] = high
        low_ref[2 * TILE :, :] = low

        for done in range(1, blocks):

            @pl.when(k == done - 1)
            def _():
                rest = slice(done * TILE, PANEL)
                work_ref[rest, (done - 1) * TILE : done * TILE] = jnp.zeros((PANEL - done * TILE, TILE), F32)
                for top in range(done * TILE, PANEL, 2 * TILE):
                    part = slice(top, min(top + 2 * TILE, PANEL))
                    near, far = slice(0, done * TILE), slice(top, PANEL)
                    work_ref[part, near] -= dot(low_ref[:, part], high_ref[:, near], TN)
                    work_ref[part, far] -= dot(low_ref[:, part], high_ref[:, far], TN)

        return carry

    lax.fori_loop(0, blocks, step, 0)


def make_inverse(columns):
    return pl.pallas_call(
        chol_kernel,
        out_shape=jax.ShapeDtypeStruct((PANEL, PANEL), F32),
        scratch_shapes=[
            pltpu.VMEM((PANEL, PANEL), F32),
            pltpu.VMEM((3 * TILE, PANEL), BF16),
            pltpu.VMEM((3 * TILE, PANEL), BF16),
        ],
        compiler_params=pltpu.CompilerParams(vmem_limit_bytes=24 << 20),
        cost_estimate=pl.CostEstimate(flops=40 * 10**9, transcendentals=1 << 20, bytes_accessed=5 << 20),
        name="cholesky",
    )(columns)


def panel_kernel(share, row_count, col_count, rows_blk, parts, pieces, place_ref, *refs):
    recv_refs, next_refs = refs[:parts], refs[parts : parts + pieces]
    (cols_ref, inv_ref, panel_ref, update_ref, feats_ref, slots_ref, high_ref, half_ref,
     own_ref, own_half_ref) = refs[parts + pieces :]
    step = pl.program_id(0)
    row_index, col_index = place_ref[0], place_ref[1]
    col_tiles = PANEL // TILE // col_count
    width = col_tiles * TILE
    groups = recv_refs[0].shape[0] * share // TILE
    total = parts * groups

    @pl.when(step == 0)
    def _():
        for p in range(parts):
            for g in range(groups):
                q = p * groups + g
                slots_ref[:, q * TILE : (q + 1) * TILE] = jnp.broadcast_to(
                    read_slots(recv_refs[p], (), share, g), (8, TILE)
                )
                feats_ref[q * TILE : (q + 1) * TILE, :] = gather_rows(recv_refs[p], (), share, g)
        half_row = as_row(half_norms(cols_ref[...]))
        half_ref[...] = jnp.broadcast_to(half_row, (8, PANEL))
        inverse = split(inv_ref[...])
        own = []
        for t in range(col_tiles):
            tile = t * col_count + col_index
            for n, next_ref in enumerate(next_refs):

                @pl.when(place_ref[2 + n] == tile)
                def _():
                    own_ref[t * TILE : (t + 1) * TILE, :] = next_ref[...]

            own.append(inv_ref[pl.ds(pl.multiple_of(tile * TILE, TILE), TILE), :])
        own_feats = own_ref[...]
        own_half = half_norms(own_feats)
        own_half_ref[...] = jnp.broadcast_to(as_row(own_half), (8, width))
        cross = rbf(own_feats, own_half, cols_ref[...], half_row)
        block = 2 * TILE
        cut = lambda pair, rows, cols: (pair[0][rows, cols], pair[1][rows, cols])
        cross = split(cross)
        halfway = []
        for n in range(0, PANEL, block):
            here, upto = slice(n, n + block), slice(0, n + block)
            halfway.append(dot_split(cut(cross, slice(None), upto), cut(inverse, here, upto), NT))
        halfway = split(jnp.concatenate(halfway, axis=1))
        solved = []
        for n in range(0, PANEL, block):
            here, below = slice(n, n + block), slice(n, PANEL)
            solved.append(dot_split(cut(halfway, slice(None), below), cut(inverse, below, here)))
        solved = jnp.concatenate(solved, axis=1)
        right = jnp.concatenate(own + [solved], axis=0)
        high, low = split(right.T)
        high_ref[0:PANEL, :] = high
        high_ref[PANEL : 2 * PANEL, :] = low
        high_ref[2 * PANEL :, :] = high

    def body(diagonal):
        slot = iota((rows_blk, TILE), 0) + step * rows_blk
        pick = jnp.concatenate(
            [one_hot(slot == slots_ref[0:1, q * TILE : (q + 1) * TILE]) for q in range(total)], axis=1
        )
        feats = dot(pick, feats_ref[...]).astype(BF16)
        half = half_norms(feats)
        kern = rbf(feats, half, cols_ref[...], half_ref[0:1, :])
        kern_next = rbf(feats, half, own_ref[...], own_half_ref[0:1, :])
        if diagonal:
            local = iota((rows_blk, 1), 0) + step * rows_blk
            place = (local // TILE * row_count + row_index) * TILE + local % TILE
            kern = kern + jnp.where(place == iota((rows_blk, PANEL), 1), noise_var, 0.0)
            index = iota((rows_blk, width), 1)
            column = PANEL + (index // TILE * col_count + col_index) * TILE + index % TILE
            kern_next = kern_next + jnp.where(place == column, noise_var, 0.0)
        high, low = split(kern)
        result = dot(jnp.concatenate([high, high, low], axis=1), high_ref[...])
        update = kern_next - result[:, width:]
        for t in range(col_tiles):
            where = pl.ds(t, rows_blk, stride=col_tiles) if col_tiles > 1 else slice(None)
            panel_ref[where, :] = result[:, t * TILE : (t + 1) * TILE]
            update_ref[where, :] = update[:, t * TILE : (t + 1) * TILE]

    lead_rows = max(2 * PANEL // row_count, TILE)
    has_diag = step * rows_blk < lead_rows

    @pl.when(has_diag)
    def _():
        body(True)

    @pl.when(jnp.logical_not(has_diag))
    def _():
        body(False)


def make_outputs(parts, pieces, piece_tiles, columns, inverse, share, row_count, col_count):
    feat = columns.shape[1]
    local_rows = len(parts) * parts[0].shape[0] * share
    col_tiles = PANEL // TILE // col_count
    width = col_tiles * TILE
    rows_blk = 512
    place = jnp.stack([lax.axis_index("row"), lax.axis_index("col")] + piece_tiles).astype(jnp.int32)
    operands = (*parts, *pieces, columns, inverse)
    out = jax.ShapeDtypeStruct((local_rows * col_tiles, TILE), F32)
    out_spec = pl.BlockSpec((rows_blk * col_tiles, TILE), lambda i, s: (i, 0))
    return pl.pallas_call(
        functools.partial(panel_kernel, share, row_count, col_count, rows_blk, len(parts), len(pieces)),
        out_shape=[out, out],
        grid_spec=pltpu.PrefetchScalarGridSpec(
            num_scalar_prefetch=1,
            grid=(local_rows // rows_blk,),
            in_specs=[pl.BlockSpec(memory_space=pltpu.VMEM)] * len(operands),
            out_specs=[out_spec, out_spec],
            scratch_shapes=[
                pltpu.VMEM((local_rows, feat), BF16),
                pltpu.VMEM((8, local_rows), jnp.int32),
                pltpu.VMEM((3 * PANEL, 2 * width), BF16),
                pltpu.VMEM((8, PANEL), F32),
                pltpu.VMEM((width, feat), BF16),
                pltpu.VMEM((8, width), F32),
            ],
        ),
        compiler_params=pltpu.CompilerParams(vmem_limit_bytes=36 << 20),
        name="panels",
    )(place, *operands)


def shift(value, axis, distance, size):
    return lax.ppermute(value, axis, [(i, (i + distance) % size) for i in range(size)])


def exchange(value, axis, step, size):
    return lax.ppermute(value, axis, [(i, i ^ step) for i in range(size)])


def sum_over(value, axis, size):
    step = 1
    while step < size:
        value = value + exchange(value, axis, step, size)
        step *= 2
    return value


def next_tiles(tile, row_count, col_count):
    turns = PANEL // TILE // col_count
    row_index, col_index = lax.axis_index("row"), lax.axis_index("col")
    pieces, piece_tiles = [], []
    for turn in range(turns):
        pairs = []
        for r in range(row_count):
            for c in range(col_count):
                owner = c + col_count * ((r // col_count + turn) % turns)
                pairs.append((owner * col_count + r % col_count, r * col_count + c))
        pieces.append(lax.ppermute(tile, ("row", "col"), pairs))
        piece_tiles.append(col_index + col_count * ((row_index // col_count + turn) % turns))
    return pieces, piece_tiles


def per_device(images, weight_in, bias_in, weight_out, feature_scale, position):
    image_rows = images.shape[0]
    feat = weight_out.shape[1]
    row_count = lax.axis_size("row")
    col_count = lax.axis_size("col")
    share = image_rows // row_count
    lead_tiles = 2 * PANEL // (TILE * row_count)
    bucket = make_features(
        images, weight_in, bias_in, weight_out, feature_scale, position, row_count
    )
    received = lax.all_to_all(bucket, "row", split_axis=0, concat_axis=0, tiled=True)
    lead = make_lead(received, share, lead_tiles)
    lead = sum_over(lead, "col", col_count)
    lead, received = lax.optimization_barrier((lead, received))
    parts = [received] + [shift(received, "col", d, col_count) for d in range(1, col_count)]
    columns = lax.all_gather(lead[:TILE], "row", axis=0, tiled=True)
    if lead_tiles > 1:
        lead, columns = lax.optimization_barrier((lead, columns))
        pieces, piece_tiles = next_tiles(lead[TILE : 2 * TILE], row_count, col_count)
    else:
        pieces = [columns[PANEL + t * TILE : PANEL + (t + 1) * TILE] for t in range(PANEL // TILE)]
        piece_tiles = [jnp.int32(t) for t in range(PANEL // TILE)]
    inverse = make_inverse(columns[:PANEL])
    panel, update = make_outputs(
        parts, pieces, piece_tiles, columns[:PANEL], inverse, share, row_count, col_count
    )
    shape_out = (image_rows * col_count // TILE, TILE, PANEL // TILE // col_count, TILE)
    return panel.reshape(shape_out), update.reshape(shape_out)


def solution(mesh):
    in_specs = (P(("row", "col"), None), P(), P(), P(), P(), P(("row", "col")))
    out_specs = (P(None, "row", None, "col"), P(None, "row", None, "col"))
    return jax.shard_map(
        per_device, mesh=mesh, in_specs=in_specs, out_specs=out_specs, check_vma=False
    )
```

```python
import functools

import jax
import jax.numpy as jnp
from jax import lax
from jax.experimental import pallas as pl
from jax.experimental.pallas import tpu as pltpu
from jax.sharding import PartitionSpec as P

TILE = 128
PANEL = 1024
META = 8
F32 = jnp.float32
BF16 = jnp.bfloat16
NN = (((1,), (0,)), ((), ()))
NT = (((1,), (1,)), ((), ()))
TN = (((0,), (0,)), ((), ()))

noise_var = 0.5


def iota(shape, dim):
    return lax.broadcasted_iota(jnp.int32, shape, dim)


def one_hot(cond):
    return jnp.where(cond, 1.0, 0.0).astype(BF16)


def dot(left, right, dims=NN):
    return lax.dot_general(left, right, dims, preferred_element_type=F32)


def split(value):
    high = value.astype(BF16)
    return high, (value - high.astype(F32)).astype(BF16)


def dot_split(left, right, dims=NN):
    return dot(left[0], right[0], dims) + (
        dot(left[0], right[1], dims) + dot(left[1], right[0], dims)
    )


def dot_stacked(left, right, dims=NN):
    side = dims[0][1][0]
    return dot(
        jnp.concatenate([left[0], left[0], left[1]], axis=1),
        jnp.concatenate([right[0], right[1], right[0]], axis=side),
        dims,
    )


def half_norms(feats):
    wide = feats.astype(F32)
    return 0.5 * jnp.sum(wide * wide, axis=1, keepdims=True)


def as_row(column):
    rows = column.shape[0]
    return jnp.broadcast_to(column, (rows, TILE)).T[:1, :]


def rbf(left, left_half, right, right_half_row):
    cross = dot(left, right, NT)
    return jnp.exp(jnp.minimum(cross - left_half - right_half_row, 0.0))


def feature_kernel(
    share, row_count, pos_ref, img_ref, win_ref, bias_ref, wout_ref, scale_ref, out_ref, acc_ref
):
    step = pl.program_id(0)
    preact = dot(img_ref[...], win_ref[...]) + bias_ref[...]
    inner = preact * (0.7978845608 + 0.7978845608 * 0.044715 * preact * preact)
    half = 0.5 * preact
    hidden = half + half * jnp.tanh(inner)
    part = dot(hidden.astype(BF16), wout_ref[...])

    @pl.when(step == 0)
    def _():
        acc_ref[...] = part

    @pl.when(step > 0)
    def _():
        acc_ref[...] += part

    @pl.when(step == pl.num_programs(0) - 1)
    def _():
        images = row_count * share
        feats = (acc_ref[...] * scale_ref[...]).astype(BF16)
        place = pos_ref[...]
        tile = place // TILE
        group = tile % row_count
        member = iota((row_count, images), 0) == group
        before = one_hot(iota((images, images), 0) < iota((images, images), 1))
        rank = dot(one_hot(member), before)
        target = jnp.where(member, rank + (share * iota((row_count, images), 0)).astype(F32), 0.0)
        target = jnp.sum(target, axis=0, keepdims=True).astype(jnp.int32)
        order = one_hot(iota((images, images), 0) == target)
        sorted_feats = dot(order, feats).astype(BF16)
        meta_row = iota((META, images), 0)
        meta = jnp.where(meta_row == 0, tile // row_count, jnp.where(meta_row == 1, place % TILE, 0))
        meta = meta.astype(F32).astype(BF16)
        lane = iota((TILE, images), 0) % share
        for r in range(row_count):
            out_ref[r, :share, :] = sorted_feats[r * share : (r + 1) * share, :]
            sel = one_hot(lane + r * share == target)
            spread = dot(meta, sel, NT).astype(BF16)
            out_ref[r, share:, :TILE] = spread
            out_ref[r, share:, TILE:] = jnp.zeros((META, out_ref.shape[2] - TILE), BF16)


def make_features(images, weight_in, bias_in, weight_out, feature_scale, position, row_count):
    rows, din = images.shape
    hid, feat = weight_out.shape
    share = rows // row_count
    block = 1024
    operands = (
        position.reshape(1, rows),
        images,
        weight_in,
        bias_in.reshape(1, hid),
        weight_out,
        feature_scale.reshape(1, feat),
    )
    return pl.pallas_call(
        functools.partial(feature_kernel, share, row_count),
        out_shape=jax.ShapeDtypeStruct((row_count, share + META, feat), BF16),
        grid=(hid // block,),
        in_specs=[
            pl.BlockSpec((1, rows), lambda i: (0, 0)),
            pl.BlockSpec((rows, din), lambda i: (0, 0)),
            pl.BlockSpec((din, block), lambda i: (0, i)),
            pl.BlockSpec((1, block), lambda i: (0, i)),
            pl.BlockSpec((block, feat), lambda i: (i, 0)),
            pl.BlockSpec((1, feat), lambda i: (0, 0)),
        ],
        out_specs=pl.BlockSpec((row_count, share + META, feat), lambda i: (0, 0, 0)),
        scratch_shapes=[pltpu.VMEM((rows, feat), F32)],
        compiler_params=pltpu.CompilerParams(vmem_limit_bytes=32 << 20),
        name="features",
    )(*[pltpu.with_memory_space_constraint(x, pltpu.HBM) for x in operands])


def read_slots(block_ref, lead, share, group):
    per = TILE // share
    lane = iota((META, TILE), 1) // share
    meta = None
    for j in range(per):
        piece = block_ref[lead + (group * per + j, slice(share, share + META), slice(0, TILE))].astype(F32)
        meta = piece if meta is None else jnp.where(lane == j, piece, meta)
    return (meta[0:1, :] * TILE + meta[1:2, :]).astype(jnp.int32)


def gather_rows(block_ref, lead, share, group):
    per = TILE // share
    return jnp.concatenate(
        [block_ref[lead + (group * per + j, slice(0, share), slice(None))] for j in range(per)], axis=0
    )


def lead_kernel(share, recv_ref, out_ref):
    groups = recv_ref.shape[0] * share // TILE
    slots = [read_slots(recv_ref, (), share, g) for g in range(groups)]
    rows = jnp.concatenate([gather_rows(recv_ref, (), share, g) for g in range(groups)], axis=0)
    shape = (out_ref.shape[0], TILE)
    pick = jnp.concatenate([one_hot(iota(shape, 0) == s) for s in slots], axis=1)
    out_ref[...] = dot(pick, rows).astype(BF16)


def make_lead(received, share, lead_tiles):
    return pl.pallas_call(
        functools.partial(lead_kernel, share),
        out_shape=jax.ShapeDtypeStruct((lead_tiles * TILE, received.shape[2]), BF16),
        name="lead",
    )(received)


def diag_inverse(block):
    size, width, ahead = block.shape[0], 8, 3
    count = size // width
    shape = (width, size)
    sub, lane = iota(shape, 0), iota(shape, 1)
    spread = lambda x: jnp.broadcast_to(x, shape)
    work = [block[q * width : (q + 1) * width, :] for q in range(count)]
    columns = {}
    out = []
    for g in range(count):
        base, first = g * width, g + ahead + 1
        rows = range(g, min(first, count))
        for q in rows:
            for h in range(g, min(q, g + 1) + 1):
                if (q, h) not in columns:
                    columns[q, h] = [spread(work[q][:, h * width + k : h * width + k + 1]) for k in range(width)]
        pivot_lane = (lane >= base) & (lane < base + width)
        for q in rows:
            start = jnp.where(lane - base == sub, 1.0, 0.0) if q == g else 0.0
            work[q] = jnp.where(pivot_lane, start, work[q])
        diag = jnp.ones(shape, F32)
        for i in range(width):
            own = spread(columns[g, g][i][i : i + 1, :])
            inv = 1.0 / own
            diag = jnp.where(sub == i, own, diag)
            source = {q: columns[q, g][i] for q in rows}
            factor = {q: source[q] * inv for q in rows}
            factor[g] = jnp.where(sub > i, factor[g], 0.0)
            for h in range(g, min(g + 2, count)):
                for k in range(i + 1 if h == g else 0, width):
                    value = spread(source[h][k : k + 1, :])
                    for q in rows:
                        if q >= h:
                            columns[q, h][k] = columns[q, h][k] - factor[q] * value
            pivot = spread(work[g][i : i + 1, :])
            for q in rows:
                work[q] = work[q] - factor[q] * pivot
        scaled = work[g] * lax.rsqrt(diag)
        out.append(jnp.where(lane < base + width, scaled, 0.0))
        if first < count:
            high = scaled.astype(BF16).astype(F32)
            low = scaled - high
            zero = jnp.zeros_like(high)
            lhs = jnp.concatenate([high, high, low, zero], axis=0).astype(BF16)
            rhs = jnp.concatenate([high, low, high, zero], axis=0).astype(BF16)
            gone = dot(lhs, rhs, TN)
            for q in range(first, count):
                work[q] = jnp.where(pivot_lane, 0.0, work[q]) - gone[q * width : (q + 1) * width, :]
    return jnp.concatenate(out, axis=0)


def chol_kernel(cols_ref, out_ref, work_ref, stack_ref):
    blocks = PANEL // TILE
    feats = cols_ref[...]
    half = half_norms(feats)
    half_row = as_row(half)
    chunk = 2 * TILE
    for top in range(0, PANEL, chunk):
        rows, cols = slice(top, top + chunk), slice(top, PANEL)
        block = rbf(feats[rows], half[rows], feats[cols], half_row[:, cols])
        eye = iota(block.shape, 0) == iota(block.shape, 1)
        work_ref[rows, cols] = block + jnp.where(eye, noise_var, 0.0)
        if top:
            work_ref[rows, :top] = jnp.zeros((chunk, top), F32)
    lane = iota((TILE, PANEL), 1)

    def step(k, carry):
        base = pl.multiple_of(k * TILE, TILE)
        inverse = diag_inverse(work_ref[pl.ds(base, TILE), pl.ds(base, TILE)])
        work_ref[pl.ds(base, TILE), pl.ds(base, TILE)] = jnp.where(
            iota((TILE, TILE), 0) == iota((TILE, TILE), 1), 1.0, 0.0
        )
        row = dot_stacked(split(inverse), split(work_ref[pl.ds(base, TILE), :]))
        out_ref[pl.ds(base, TILE), :] = jnp.where(lane < base + TILE, row, 0.0)
        high, low = split(row)
        stack_ref[:TILE, :] = high
        stack_ref[TILE : 2 * TILE, :] = low
        stack_ref[2 * TILE :, :] = high

        for done in range(1, blocks):

            @pl.when(k == done - 1)
            def _():
                rest = slice(done * TILE, PANEL)
                work_ref[rest, (done - 1) * TILE : done * TILE] = jnp.zeros((PANEL - done * TILE, TILE), F32)
                turned = [x[:, rest].T for x in (high, low)]
                lower = jnp.concatenate([turned[0], turned[0], turned[1]], axis=1)
                for n in range(0, PANEL, 2 * TILE):
                    cols = slice(n, n + 2 * TILE)
                    stop = PANEL if n < done * TILE else n + 2 * TILE
                    mine = lower[: stop - done * TILE]
                    work_ref[done * TILE : stop, cols] -= dot(mine, stack_ref[:, cols])

        return carry

    lax.fori_loop(0, blocks, step, 0)


def make_inverse(columns):
    return pl.pallas_call(
        chol_kernel,
        out_shape=jax.ShapeDtypeStruct((PANEL, PANEL), F32),
        scratch_shapes=[
            pltpu.VMEM((PANEL, PANEL), F32),
            pltpu.VMEM((3 * TILE, PANEL), BF16),
        ],
        compiler_params=pltpu.CompilerParams(vmem_limit_bytes=24 << 20),
        cost_estimate=pl.CostEstimate(flops=40 * 10**9, transcendentals=1 << 20, bytes_accessed=5 << 20),
        name="cholesky",
    )(columns)


def panel_kernel(share, row_count, col_count, rows_blk, parts, pieces, place_ref, *refs):
    recv_refs, next_refs = refs[:parts], refs[parts : parts + pieces]
    (cols_ref, inv_ref, panel_ref, update_ref, feats_ref, slots_ref, high_ref, half_ref,
     own_ref, own_half_ref) = refs[parts + pieces :]
    step = pl.program_id(0)
    row_index, col_index = place_ref[0], place_ref[1]
    col_tiles = PANEL // TILE // col_count
    width = col_tiles * TILE
    groups = recv_refs[0].shape[0] * share // TILE
    total = parts * groups

    @pl.when(step == 0)
    def _():
        for p in range(parts):
            for g in range(groups):
                q = p * groups + g
                slots_ref[:, q * TILE : (q + 1) * TILE] = jnp.broadcast_to(
                    read_slots(recv_refs[p], (), share, g), (8, TILE)
                )
                feats_ref[q * TILE : (q + 1) * TILE, :] = gather_rows(recv_refs[p], (), share, g)
        half_row = as_row(half_norms(cols_ref[...]))
        half_ref[...] = jnp.broadcast_to(half_row, (8, PANEL))
        inverse = split(inv_ref[...])
        own = []
        for t in range(col_tiles):
            tile = t * col_count + col_index
            for n, next_ref in enumerate(next_refs):

                @pl.when(place_ref[2 + n] == tile)
                def _():
                    own_ref[t * TILE : (t + 1) * TILE, :] = next_ref[...]

            own.append(inv_ref[pl.ds(pl.multiple_of(tile * TILE, TILE), TILE), :])
        own_feats = own_ref[...]
        own_half = half_norms(own_feats)
        own_half_ref[...] = jnp.broadcast_to(as_row(own_half), (8, width))
        cross = rbf(own_feats, own_half, cols_ref[...], half_row)
        block = 2 * TILE
        cut = lambda pair, rows, cols: (pair[0][rows, cols], pair[1][rows, cols])
        cross = split(cross)
        halfway = []
        for n in range(0, PANEL, block):
            here, upto = slice(n, n + block), slice(0, n + block)
            halfway.append(dot_stacked(cut(cross, slice(None), upto), cut(inverse, here, upto), NT))
        halfway = split(jnp.concatenate(halfway, axis=1))
        solved = []
        for n in range(0, PANEL, block):
            here, below = slice(n, n + block), slice(n, PANEL)
            solved.append(dot_stacked(cut(halfway, slice(None), below), cut(inverse, below, here)))
        solved = jnp.concatenate(solved, axis=1)
        right = jnp.concatenate(own + [solved], axis=0)
        high, low = split(right.T)
        high_ref[0:PANEL, :] = high
        high_ref[PANEL : 2 * PANEL, :] = low
        high_ref[2 * PANEL :, :] = high

    def body(diagonal):
        slot = iota((rows_blk, TILE), 0) + step * rows_blk
        pick = jnp.concatenate(
            [one_hot(slot == slots_ref[0:1, q * TILE : (q + 1) * TILE]) for q in range(total)], axis=1
        )
        feats = dot(pick, feats_ref[...]).astype(BF16)
        half = half_norms(feats)
        kern = rbf(feats, half, cols_ref[...], half_ref[0:1, :])
        kern_next = rbf(feats, half, own_ref[...], own_half_ref[0:1, :])
        if diagonal:
            local = iota((rows_blk, 1), 0) + step * rows_blk
            place = (local // TILE * row_count + row_index) * TILE + local % TILE
            kern = kern + jnp.where(place == iota((rows_blk, PANEL), 1), noise_var, 0.0)
            index = iota((rows_blk, width), 1)
            column = PANEL + (index // TILE * col_count + col_index) * TILE + index % TILE
            kern_next = kern_next + jnp.where(place == column, noise_var, 0.0)
        high, low = split(kern)
        result = dot(jnp.concatenate([high, high, low], axis=1), high_ref[...])
        update = kern_next - result[:, width:]
        for t in range(col_tiles):
            where = pl.ds(t, rows_blk, stride=col_tiles) if col_tiles > 1 else slice(None)
            panel_ref[where, :] = result[:, t * TILE : (t + 1) * TILE]
            update_ref[where, :] = update[:, t * TILE : (t + 1) * TILE]

    lead_rows = max(2 * PANEL // row_count, TILE)
    has_diag = step * rows_blk < lead_rows

    @pl.when(has_diag)
    def _():
        body(True)

    @pl.when(jnp.logical_not(has_diag))
    def _():
        body(False)


def make_outputs(parts, pieces, piece_tiles, columns, inverse, share, row_count, col_count):
    feat = columns.shape[1]
    local_rows = len(parts) * parts[0].shape[0] * share
    col_tiles = PANEL // TILE // col_count
    width = col_tiles * TILE
    rows_blk = 512
    place = jnp.stack([lax.axis_index("row"), lax.axis_index("col")] + piece_tiles).astype(jnp.int32)
    operands = (*parts, *pieces, columns, inverse)
    out = jax.ShapeDtypeStruct((local_rows * col_tiles, TILE), F32)
    out_spec = pl.BlockSpec((rows_blk * col_tiles, TILE), lambda i, s: (i, 0))
    return pl.pallas_call(
        functools.partial(panel_kernel, share, row_count, col_count, rows_blk, len(parts), len(pieces)),
        out_shape=[out, out],
        grid_spec=pltpu.PrefetchScalarGridSpec(
            num_scalar_prefetch=1,
            grid=(local_rows // rows_blk,),
            in_specs=[pl.BlockSpec(memory_space=pltpu.VMEM)] * len(operands),
            out_specs=[out_spec, out_spec],
            scratch_shapes=[
                pltpu.VMEM((local_rows, feat), BF16),
                pltpu.VMEM((8, local_rows), jnp.int32),
                pltpu.VMEM((3 * PANEL, 2 * width), BF16),
                pltpu.VMEM((8, PANEL), F32),
                pltpu.VMEM((width, feat), BF16),
                pltpu.VMEM((8, width), F32),
            ],
        ),
        compiler_params=pltpu.CompilerParams(vmem_limit_bytes=36 << 20),
        name="panels",
    )(place, *operands)


def shift(value, axis, distance, size):
    return lax.ppermute(value, axis, [(i, (i + distance) % size) for i in range(size)])


def exchange(value, axis, step, size):
    return lax.ppermute(value, axis, [(i, i ^ step) for i in range(size)])


def sum_over(value, axis, size):
    step = 1
    while step < size:
        value = value + exchange(value, axis, step, size)
        step *= 2
    return value


def next_tiles(tile, row_count, col_count):
    turns = PANEL // TILE // col_count
    row_index, col_index = lax.axis_index("row"), lax.axis_index("col")
    pieces, piece_tiles = [], []
    for turn in range(turns):
        pairs = []
        for r in range(row_count):
            for c in range(col_count):
                owner = c + col_count * ((r // col_count + turn) % turns)
                pairs.append((owner * col_count + r % col_count, r * col_count + c))
        pieces.append(lax.ppermute(tile, ("row", "col"), pairs))
        piece_tiles.append(col_index + col_count * ((row_index // col_count + turn) % turns))
    return pieces, piece_tiles


def per_device(images, weight_in, bias_in, weight_out, feature_scale, position):
    image_rows = images.shape[0]
    feat = weight_out.shape[1]
    row_count = lax.axis_size("row")
    col_count = lax.axis_size("col")
    share = image_rows // row_count
    lead_tiles = 2 * PANEL // (TILE * row_count)
    bucket = make_features(
        images, weight_in, bias_in, weight_out, feature_scale, position, row_count
    )
    received = lax.all_to_all(bucket, "row", split_axis=0, concat_axis=0, tiled=True)
    lead = make_lead(received, share, lead_tiles)
    lead = sum_over(lead, "col", col_count)
    lead, received = lax.optimization_barrier((lead, received))
    parts = [received] + [shift(received, "col", d, col_count) for d in range(1, col_count)]
    columns = lax.all_gather(lead[:TILE], "row", axis=0, tiled=True)
    if lead_tiles > 1:
        lead, columns = lax.optimization_barrier((lead, columns))
        pieces, piece_tiles = next_tiles(lead[TILE : 2 * TILE], row_count, col_count)
    else:
        pieces = [columns[PANEL + t * TILE : PANEL + (t + 1) * TILE] for t in range(PANEL // TILE)]
        piece_tiles = [jnp.int32(t) for t in range(PANEL // TILE)]
    inverse = make_inverse(columns[:PANEL])
    panel, update = make_outputs(
        parts, pieces, piece_tiles, columns[:PANEL], inverse, share, row_count, col_count
    )
    shape_out = (image_rows * col_count // TILE, TILE, PANEL // TILE // col_count, TILE)
    return panel.reshape(shape_out), update.reshape(shape_out)


def solution(mesh):
    in_specs = (P(("row", "col"), None), P(), P(), P(), P(), P(("row", "col")))
    out_specs = (P(None, "row", None, "col"), P(None, "row", None, "col"))
    return jax.shard_map(
        per_device, mesh=mesh, in_specs=in_specs, out_specs=out_specs, check_vma=False
    )
```
